128 devices in a mesh: img: 32 (over x, y, core), tok: 4 (over z).
Axes of the slice: x: 4, y: 4, z: 4, core: 2. Of those that a mesh axis runs over, the one named last changes fastest.
Arguments:
- tokens: bfloat16 [32, 4096, 1280], P('img', 'tok'), may hold values from -8 to 8
- ln_gain: float32 [1280], replicated, may hold values from 0.25 to 1.75
- w_qkv: bfloat16 [1280, 1920], replicated, may hold values from -2 to 2
- w_proj: bfloat16 [640, 1280], replicated, may hold values from -0.25 to 0.25
- w_neck1: bfloat16 [1280, 256], replicated, may hold values from -0.15625 to 0.15625
- neck_gain1: float32 [256], replicated, may hold values from 0.25 to 1.75
- w_neck2: bfloat16 [2304, 256], replicated, may hold values from -0.125 to 0.125
- neck_gain2: float32 [256], replicated, may hold values from 0.25 to 1.75
- pe_matrix: float32 [2, 128], replicated, may hold values from -6 to 6
- query_bias: float32 [256], replicated, may hold values from -6 to 6
- dec_qkv: float32 [3, 256, 128], replicated, may hold values from -2 to 2
- dec_out: float32 [128, 256], replicated, may hold values from -0.5 to 0.5
- dec_gains: float32 [2, 256], replicated, may hold values from 0.25 to 1.75
- w_mlp1: float32 [256, 2048], replicated, may hold values from -0.375 to 0.375
- w_mlp2: float32 [2048, 256], replicated, may hold values from -0.1875 to 0.1875
- w_hyper: float32 [2, 256, 256], replicated, may hold values from -0.5 to 0.5
- w_hyper_out: float32 [256, 32], replicated, may hold values from -0.5 to 0.5
- w_up1: float32 [256, 256], replicated, may hold values from -0.375 to 0.375
- up_gain: float32 [64], replicated, may hold values from 0.25 to 1.75
- w_up2: float32 [64, 128], replicated, may hold values from -0.75 to 0.75
- req_image: int32 [2048, 1], P('img'), may hold values from 0 to 31; in each aligned block of 64 rows (0 to 63, 64 to 127, ...) at most 4 rows name the same one
- points: int32 [2048, 2], P('img'), may hold values from 0 to 1023
Outputs:
- masks: float32 [2048, 65536], P('img', 'tok')
The draws below stay inside these ranges and needn't reach their ends.
Inputs may be any that keep to these rules, and one draw needn't show every extreme that they name: `req_image`: among the 64 rows of one owner no image is named more than 4 times; in some owner's rows an image is named exactly 4 times.
All inputs are finite; a program needn't handle non-finite values.
Results may differ from the reference program's by a relative error of at most 0.035.
Values may be sent and summed in bfloat16 or wider, within the bound.
A program may use at most 320 MiB of HBM per device.

```python
import math
import jax
import jax.numpy as jnp
import numpy as np
from jax import lax

WIDTH = 1280
HEADS = 8
HDIM = 80
GRID = 64
NECK = 256
ATTN_DIM = 128
DEC_HEADS = 8
MLP_DIM = 2048
UP1 = 64
UP2 = 32
IMG_SIDE = 1024
TOKENS = 4096
N_IMAGES = 32
SLOTS = 64
CAP = 4
N_IMG = 32


def draw_tokens(key, part):
    drawn_draw = jax.random.normal(jax.random.fold_in(key, 17), (N_IMAGES, TOKENS, WIDTH), jnp.float32)
    return jnp.clip(drawn_draw, -6.0, 6.0).astype(jnp.bfloat16)


def draw_w_qkv(key, part):
    spread = (WIDTH // 4) ** (-0.5)
    drawn_draw = jnp.clip(jax.random.normal(jax.random.fold_in(key, 21), (WIDTH, 3 * HEADS * HDIM), jnp.float32), -5.0, 5.0) * spread
    return jnp.clip(drawn_draw, -2.0, 2.0).astype(jnp.bfloat16)


def draw_query_bias(key, part):
    drawn_draw = jnp.clip(jax.random.normal(jax.random.fold_in(key, 31), (NECK,), jnp.float32), -6.0, 6.0)
    return jnp.clip(drawn_draw, -6.0, 6.0)


def draw_dec_qkv(key, part):
    spread = (NECK // 4) ** (-0.5)
    drawn_draw = jnp.clip(jax.random.normal(jax.random.fold_in(key, 41), (3, NECK, ATTN_DIM), jnp.float32), -5.0, 5.0) * spread
    return jnp.clip(drawn_draw, -2.0, 2.0)


def set_ends(entries, own_key, low, largest):
    longest = entries.shape.index(max(entries.shape))
    spots = []
    for shift in (0, 1):
        where = [jax.random.randint(jax.random.fold_in(own_key, axis), (), 0, length) for axis, length in enumerate(entries.shape)]
        where[longest] = (where[longest] + shift) % entries.shape[longest]
        spots.append(tuple(where))
    return entries.at[spots[0]].set(low).at[spots[1]].set(largest)


def deal_out(key, own, number, rows, number_of, top, bound, slope):
    sequence = jax.random.permutation(key, number_of)
    crowded, usual = shares(number_of, rows * top, bound, slope, True), shares(number_of, rows * top, bound, slope, False)
    places = jnp.arange(number_of)

    def named(tallies, rotation):
        used = int((tallies > 0).sum())
        fixed = max(1, used // 4)
        shifted = fixed + (places - fixed + rotation * (used - fixed)) % max(1, number_of - fixed)
        return jnp.zeros((number_of,), jnp.int32).at[sequence[jnp.where(places < fixed, places, shifted)]].set(jnp.asarray(tallies, jnp.int32))

    tallies = jnp.where(number % 4 == 0, named(crowded, number // 4), named(usual, number - number // 4 - 1))
    mixed = jax.random.permutation(jax.random.fold_in(own, 3), number_of)
    source_of, taker = mixed[0:number_of // 2 * 2:2], mixed[1:number_of // 2 * 2:2]
    slack = jnp.minimum(tallies[source_of] - 1, bound - tallies[taker]) // 2
    slack = jnp.where((source_of == sequence[0]) | (taker == sequence[0]) | (tallies[taker] == 0), 0, jnp.maximum(slack, 0))
    shifted = jax.random.randint(jax.random.fold_in(own, 4), (number_of // 2,), 0, 1 << 20) % (slack + 1)
    tallies = tallies.at[source_of].add(-shifted).at[taker].add(shifted)
    members = jnp.searchsorted(jnp.cumsum(tallies), jnp.arange(rows * top), side="right").astype(jnp.int32)
    listing = members.reshape(top, rows).T
    listing = listing[jax.random.permutation(jax.random.fold_in(own, 1), rows)]
    rotation = jax.random.randint(jax.random.fold_in(own, 2), (rows, 1), 0, top)
    return jnp.take_along_axis(listing, (jnp.arange(top)[None, :] + rotation) % top, axis=1)


def shares(number_of, total, most, slope, full):
    loads = [(1 << 20) // math.isqrt(grade ** slope) + 1 for grade in range(1, number_of + 1)]
    largest = most if full else min(most, max(-(-total // number_of), total * loads[0] // sum(loads)))
    least = 1 if total - largest >= number_of - 1 else 0
    counts, surplus = [largest] + [least] * (number_of - 1), total - largest - least * (number_of - 1)
    while surplus > 0:
        movable = [i for i in range(1, number_of) if counts[i] < largest] or [i for i in range(1, number_of) if counts[i] < most]
        pool, left = sum([loads[i] for i in movable]), surplus
        for i in movable:
            extra = min(most - counts[i], max(1, left * loads[i] // pool), surplus)
            counts[i] = counts[i] + extra
            surplus = surplus - extra
    return np.array(counts)


def scatter_about(rng, dims, scale, reach, held_as=jnp.bfloat16):
    drawn = jax.random.normal(rng, dims, jnp.float32) * scale
    return jnp.minimum(jnp.maximum(drawn, -reach), reach).astype(held_as)


def setup_inputs(seed: int = 0) -> dict:
    arg_keys = jax.random.split(jax.random.key(seed), 23)
    tokens = draw_tokens(jax.random.fold_in(arg_keys[22], 71), 0)
    ln_gain = jnp.clip(1.0 + 0.15 * jax.random.normal(arg_keys[1], (WIDTH,), jnp.float32), 0.25, 1.75)
    w_qkv = draw_w_qkv(jax.random.fold_in(arg_keys[22], 71), 0)
    w_proj = scatter_about(arg_keys[3], (HEADS * HDIM, WIDTH), (HEADS * HDIM) ** -0.5, 0.25)
    w_neck1 = scatter_about(arg_keys[4], (WIDTH, NECK), WIDTH ** -0.5, 0.15625)
    neck_gain1 = jnp.clip(1.0 + 0.15 * jax.random.normal(arg_keys[5], (NECK,), jnp.float32), 0.25, 1.75)
    w_neck2 = scatter_about(arg_keys[6], (9 * NECK, NECK), (9 * NECK) ** -0.5, 0.125)
    neck_gain2 = jnp.clip(1.0 + 0.15 * jax.random.normal(arg_keys[7], (NECK,), jnp.float32), 0.25, 1.75)
    pe_matrix = scatter_about(arg_keys[8], (2, NECK // 2), 1.0, 6.0, jnp.float32)
    query_bias = draw_query_bias(jax.random.fold_in(arg_keys[22], 71), 0)
    dec_qkv = draw_dec_qkv(jax.random.fold_in(arg_keys[22], 71), 0)
    dec_out = scatter_about(arg_keys[11], (ATTN_DIM, NECK), ATTN_DIM ** -0.5, 0.5, jnp.float32)
    dec_gains = jnp.clip(1.0 + 0.15 * jax.random.normal(arg_keys[12], (2, NECK), jnp.float32), 0.25, 1.75)
    w_mlp1 = scatter_about(arg_keys[13], (NECK, MLP_DIM), NECK ** -0.5, 0.375, jnp.float32)
    w_mlp2 = scatter_about(arg_keys[14], (MLP_DIM, NECK), (MLP_DIM // 2) ** -0.5, 0.1875, jnp.float32)
    w_hyper = scatter_about(arg_keys[15], (2, NECK, NECK), (NECK // 2) ** -0.5, 0.5, jnp.float32)
    w_hyper_out = scatter_about(arg_keys[16], (NECK, UP2), (NECK // 2) ** -0.5, 0.5, jnp.float32)
    w_up1 = scatter_about(arg_keys[17], (NECK, 4 * UP1), NECK ** -0.5, 0.375, jnp.float32)
    up_gain = jnp.clip(1.0 + 0.15 * jax.random.normal(arg_keys[18], (UP1,), jnp.float32), 0.25, 1.75)
    w_up2 = scatter_about(arg_keys[19], (UP1, 4 * UP2), UP1 ** -0.5, 0.75, jnp.float32)
    req_image_keys = jax.random.split(jax.random.fold_in(arg_keys[20], 1), (N_IMAGES * SLOTS) // SLOTS)
    req_image_turns = jax.random.permutation(jax.random.fold_in(arg_keys[20], 3), (N_IMAGES * SLOTS) // SLOTS)
    req_image = jax.vmap(lambda own, number: deal_out(jax.random.fold_in(arg_keys[20], 2), own, number, SLOTS, N_IMG, 1, CAP, 2))(req_image_keys, req_image_turns).reshape((N_IMAGES * SLOTS, 1))
    points = set_ends(jax.random.randint(arg_keys[21], (N_IMAGES * SLOTS, 2), 0, IMG_SIDE), jax.random.fold_in(arg_keys[21], 1), 0, IMG_SIDE - 1).astype(jnp.int32)
    return {"tokens": tokens, "ln_gain": ln_gain, "w_qkv": w_qkv, "w_proj": w_proj, "w_neck1": w_neck1, "neck_gain1": neck_gain1, "w_neck2": w_neck2, "neck_gain2": neck_gain2, "pe_matrix": pe_matrix, "query_bias": query_bias, "dec_qkv": dec_qkv, "dec_out": dec_out, "dec_gains": dec_gains, "w_mlp1": w_mlp1, "w_mlp2": w_mlp2, "w_hyper": w_hyper, "w_hyper_out": w_hyper_out, "w_up1": w_up1, "up_gain": up_gain, "w_up2": w_up2, "req_image": req_image, "points": points}


highest_precision = lax.Precision.HIGHEST

def layer_norm(tensor, gain_vec, epsilon):
    average = lax.optimization_barrier(jnp.mean(tensor, axis=-1, keepdims=True))
    centred = tensor - average
    spread = lax.optimization_barrier(jnp.mean(centred * centred, axis=-1, keepdims=True))
    return centred * lax.rsqrt(spread + epsilon) * gain_vec

def fourier(coords, pe_matrix):
    angles = 2.0 * math.pi * jnp.dot(coords, pe_matrix, precision=highest_precision)
    return jnp.concatenate([jnp.sin(angles), jnp.cos(angles)], axis=-1)

def grid_codes(first_row, grid_rows, pe_matrix):
    row_ids = (first_row + jnp.arange(grid_rows, dtype=jnp.int32)).astype(jnp.float32)
    col_ids = jnp.arange(GRID, dtype=jnp.int32).astype(jnp.float32)
    ycoord = (row_ids + 0.5) / GRID * 2.0 - 1.0
    xcoord = (col_ids + 0.5) / GRID * 2.0 - 1.0
    coords = jnp.stack([jnp.broadcast_to(xcoord[None, :], (grid_rows, GRID)), jnp.broadcast_to(ycoord[:, None], (grid_rows, GRID))], axis=-1)
    return fourier(coords.reshape(grid_rows * GRID, 2), pe_matrix)

def attention_core(projected, heads):
    length = projected.shape[0]
    inner_width = heads * HDIM
    factor = 1.0 / math.sqrt(HDIM)
    block_rows = min(length, 1024)

    def one_head(head_no):
        offset = (head_no * HDIM).astype(jnp.int32)
        query_matrix = lax.dynamic_slice_in_dim(projected, offset, HDIM, 1)
        key_rows = lax.dynamic_slice_in_dim(projected, offset + inner_width, HDIM, 1)
        values = lax.dynamic_slice_in_dim(projected, offset + 2 * inner_width, HDIM, 1)
        pieces = []
        for first_query in range(0, length, block_rows):
            query_rows = query_matrix[first_query:first_query + block_rows]
            attention_scores = lax.dot_general(query_rows, key_rows, (((1,), (1,)), ((), ())), preferred_element_type=jnp.float32) * factor
            maxima = lax.optimization_barrier(jnp.max(attention_scores, axis=1, keepdims=True))
            attention_weights = jnp.exp(attention_scores - maxima)
            totals = lax.optimization_barrier(jnp.sum(attention_weights, axis=1, keepdims=True))
            mixed_values = jnp.dot(attention_weights.astype(jnp.bfloat16), values, preferred_element_type=jnp.float32)
            pieces.append(mixed_values / totals)
        return jnp.concatenate(pieces, axis=0).astype(jnp.bfloat16)
    stacked = lax.map(one_head, jnp.arange(heads, dtype=jnp.int32))
    return jnp.transpose(stacked, (1, 0, 2)).reshape(length, inner_width)

def upscale(embedding, grid_rows, w_up1, up_gain, w_up2):
    first_out = jnp.dot(embedding, w_up1, precision=highest_precision).reshape(grid_rows * GRID * 4, UP1)
    first_out = jax.nn.gelu(layer_norm(first_out, up_gain, 1e-06), approximate=False)
    second = jax.nn.gelu(jnp.dot(first_out, w_up2, precision=highest_precision), approximate=False)
    second = second.reshape(grid_rows, GRID, 2, 2, 2, 2, UP2)
    second = jnp.transpose(second, (6, 0, 2, 4, 1, 3, 5))
    return second.reshape(UP2, grid_rows * GRID * 16)

def token_side(query_tok, attended, dec_out, dec_gains, w_mlp1, w_mlp2, w_hyper, w_hyper_out):
    first_out = layer_norm(query_tok + jnp.dot(attended, dec_out, precision=highest_precision), dec_gains[0], 1e-05)
    hidden = jax.nn.relu(jnp.dot(first_out, w_mlp1, precision=highest_precision))
    second = layer_norm(first_out + jnp.dot(hidden, w_mlp2, precision=highest_precision), dec_gains[1], 1e-05)
    hyper_vec = jax.nn.relu(jnp.dot(second, w_hyper[0], precision=highest_precision))
    hyper_vec = jax.nn.relu(jnp.dot(hyper_vec, w_hyper[1], precision=highest_precision))
    return jnp.dot(hyper_vec, w_hyper_out, precision=highest_precision)

def reference(tokens, ln_gain, w_qkv, w_proj, w_neck1, neck_gain1, w_neck2, neck_gain2, pe_matrix, query_bias, dec_qkv, dec_out, dec_gains, w_mlp1, w_mlp2, w_hyper, w_hyper_out, w_up1, up_gain, w_up2, req_image, points):

    def encode_one(picture):
        normed = layer_norm(picture.astype(jnp.float32), ln_gain, 1e-06).astype(jnp.bfloat16)
        projected = jnp.dot(normed, w_qkv, preferred_element_type=jnp.float32).astype(jnp.bfloat16)
        attended = attention_core(projected, HEADS)
        block_out = (picture.astype(jnp.float32) + jnp.dot(attended, w_proj, preferred_element_type=jnp.float32)).astype(jnp.bfloat16)
        narrow = layer_norm(jnp.dot(block_out, w_neck1, preferred_element_type=jnp.float32), neck_gain1, 1e-06)
        narrow = narrow.astype(jnp.bfloat16).reshape(GRID, GRID, NECK)
        framed = jnp.pad(narrow, ((1, 1), (1, 1), (0, 0)))
        columns = jnp.concatenate([framed[row_off:row_off + GRID, col_off:col_off + GRID] for row_off in range(3) for col_off in range(3)], axis=-1)
        columns = columns.reshape(TOKENS, 9 * NECK)
        embedding = layer_norm(jnp.dot(columns, w_neck2, preferred_element_type=jnp.float32), neck_gain2, 1e-06)
        positional = grid_codes(0, GRID, pe_matrix)
        dec_keys = jnp.dot(embedding + positional, dec_qkv[1], precision=highest_precision)
        dec_values = jnp.dot(embedding, dec_qkv[2], precision=highest_precision)
        upscaled = upscale(embedding, GRID, w_up1, up_gain, w_up2)
        return (dec_keys, dec_values, upscaled)
    keys_all, values_all, upscaled_all = lax.map(encode_one, tokens)
    head_size = ATTN_DIM // DEC_HEADS
    decoder_scale = 1.0 / math.sqrt(head_size)

    def decode_one(request):
        picture_no = req_image[request, 0]
        located = points[request].astype(jnp.float32)
        query_tok = query_bias + fourier(((located + 0.5) / IMG_SIDE * 2.0 - 1.0)[None, :], pe_matrix)
        query_matrix = jnp.dot(query_tok, dec_qkv[0], precision=highest_precision).reshape(DEC_HEADS, head_size)
        key_projected = keys_all[picture_no].reshape(TOKENS, DEC_HEADS, head_size)
        value_projected = values_all[picture_no].reshape(TOKENS, DEC_HEADS, head_size)
        attention_scores = jnp.einsum('hd,khd->hk', query_matrix, key_projected, precision=highest_precision) * decoder_scale
        maxima = lax.optimization_barrier(jnp.max(attention_scores, axis=1, keepdims=True))
        attention_weights = jnp.exp(attention_scores - maxima)
        mixed_values = jnp.einsum('hk,khd->hd', attention_weights, value_projected, precision=highest_precision) / lax.optimization_barrier(jnp.sum(attention_weights, axis=1))[:, None]
        hyper_vec = token_side(query_tok, mixed_values.reshape(1, ATTN_DIM), dec_out, dec_gains, w_mlp1, w_mlp2, w_hyper, w_hyper_out)
        return jnp.dot(hyper_vec, upscaled_all[picture_no], precision=highest_precision)[0]
    return lax.map(decode_one, jnp.arange(N_IMG * SLOTS, dtype=jnp.int32))
```

```python
import functools
import math

import jax
import jax.numpy as jnp
from jax import lax
from jax.experimental import pallas as pl
from jax.experimental.pallas import tpu as pltpu
from jax.sharding import PartitionSpec as P

HEADS = 8
HDIM = 80
GRID = 64
NECK = 256
ATTN_DIM = 128
DEC_HEADS = 8
UP1 = 64
UP2 = 32
IMG_SIDE = 1024
CAP = 4
MESH = pl.DeviceIdType.MESH
bf16 = jnp.bfloat16
f32 = jnp.float32
RING = 4


highest_precision = lax.Precision.HIGHEST


def norm_rows(x, gain, eps):
    centred = x - jnp.mean(x, axis=-1, keepdims=True)
    spread = jnp.mean(centred * centred, axis=-1, keepdims=True)
    return centred * lax.rsqrt(spread + eps) * gain


def encoder_kernel(
    tok_hbm, gain_ref, wqkv_hbm, wproj_hbm, wn1_hbm, g1_ref, wn2_hbm, g2_ref,
    emb_ref,
    tok, wqkv, wproj, wn1, wn2, normed, loc, got, vrows, outs, att, maps,
    halo, load_sem, qkv_send, qkv_recv, out_send, out_recv, halo_send, halo_recv,
):
    me = lax.axis_index("tok")
    rows = tok.shape[0]
    two = 2 * HDIM
    inner = HEADS * HDIM
    tile = 256
    tiles = rows // tile
    qblock = 512

    loads = [
        pltpu.make_async_copy(tok_hbm.at[pl.ds(i * tile, tile)], tok.at[pl.ds(i * tile, tile)], load_sem.at[i])
        for i in range(tiles)
    ]
    loads.append(pltpu.make_async_copy(wqkv_hbm, wqkv, load_sem.at[4]))
    loads.append(pltpu.make_async_copy(wn1_hbm, wn1, load_sem.at[5]))
    loads.append(pltpu.make_async_copy(wn2_hbm, wn2, load_sem.at[6]))
    for d in range(RING):
        owner = lax.rem(me + d, RING)
        loads.append(
            pltpu.make_async_copy(
                wproj_hbm.at[pl.ds(pl.multiple_of(owner * two, 32), two)],
                wproj.at[pl.ds(d * two, two)],
                load_sem.at[7 + d],
            )
        )
    for load in loads:
        load.start()

    barrier = pltpu.get_barrier_semaphore()
    for d in range(1, RING):
        pl.semaphore_signal(
            barrier, inc=1, device_id={"tok": lax.rem(me + d, RING)}, device_id_type=MESH
        )
    pl.semaphore_wait(barrier, RING - 1)

    for i in range(tiles):
        loads[i].wait()
        span = pl.ds(i * tile, tile)
        normed[span, :] = norm_rows(tok[span, :].astype(f32), gain_ref[...], 1e-06).astype(bf16)
    loads[4].wait()

    scale = math.log2(math.e) / math.sqrt(HDIM)

    def qkv_copy(kind, head, d):
        owner = lax.rem(me + d, RING)
        first = pl.multiple_of(kind * inner + owner * two + head * HDIM, 16)
        return pltpu.make_async_remote_copy(
            src_ref=loc.at[pl.ds(first, HDIM)],
            dst_ref=got.at[kind, head, d],
            send_sem=qkv_send.at[kind, head, d],
            recv_sem=qkv_recv.at[kind, head, d],
            device_id={"tok": owner},
            device_id_type=MESH,
        )

    def project(kind):
        @pl.loop(0, tiles)
        def _(i):
            span = pl.ds(pl.multiple_of(i * tile, tile), tile)
            part = jnp.dot(
                normed[span, :], wqkv[:, kind * inner : (kind + 1) * inner], preferred_element_type=f32
            )
            if kind == 0:
                part = part * scale
            loc[kind * inner : (kind + 1) * inner, span] = part.astype(bf16).T

    for kind in (1, 2, 0):
        project(kind)
        for d in (1, 3, 2):
            qkv_copy(kind, 0, d).start()
    for kind in (1, 2, 0):
        for d in (1, 3, 2):
            qkv_copy(kind, 1, d).start()
    for kind in range(3):
        for head in range(2):
            first = pl.multiple_of(kind * inner + me * two + head * HDIM, 16)
            got[kind, head, 0] = loc[pl.ds(first, HDIM), :]

    def out_copy(head, d):
        target = lax.rem(me - d + RING, RING)
        return pltpu.make_async_remote_copy(
            src_ref=outs.at[head, d],
            dst_ref=att.at[d, pl.ds(pl.multiple_of(head * HDIM, 16), HDIM)],
            send_sem=out_send.at[head, d],
            recv_sem=out_recv.at[head, d],
            device_id={"tok": target},
            device_id_type=MESH,
        )

    filler = (lax.broadcasted_iota(jnp.int32, (48, rows), 0) == 0).astype(bf16)
    halves = rows // qblock

    @pl.loop(0, 2)
    def _(head):
        for d in range(1, RING):
            qkv_copy(1, head, d).wait_recv()
            qkv_copy(2, head, d).wait_recv()
        for d in range(RING):
            vrows[d] = jnp.concatenate([got[2, head, d], filler], axis=0).T

        @pl.loop(0, RING)
        def _(turn):
            slot = lax.rem(turn + head, RING)

            @pl.when(slot > 0)
            def _():
                qkv_copy(0, head, slot).wait_recv()

            @pl.loop(0, halves)
            def _(half):
                span = pl.ds(pl.multiple_of(half * qblock, qblock), qblock)
                query = got[0, head, slot, :, span].T

                def scores(d):
                    return jnp.dot(query, got[1, head, d], preferred_element_type=f32)

                now = scores(0)
                top = None
                for d in range(RING):
                    ahead = scores(d + 1) if d + 1 < RING else None
                    here = jnp.max(now, axis=1, keepdims=True)
                    fresh = here if top is None else jnp.maximum(top, here)
                    weights = jnp.exp2(now - fresh).astype(bf16)
                    part = jnp.dot(weights, vrows[d], preferred_element_type=f32)
                    total = part if top is None else total * jnp.exp2(top - fresh) + part
                    top, now = fresh, ahead
                final = (total * (1.0 / total[:, HDIM : HDIM + 1])).astype(bf16).T[:HDIM]
                outs[head, slot, :, span] = final

            @pl.when(slot > 0)
            def _():
                out_copy(head, slot).start()

            @pl.when(slot == 0)
            def _():
                att[0, pl.ds(pl.multiple_of(head * HDIM, 16), HDIM), :] = outs[head, 0]

    for d in range(1, RING):
        for head in range(2):
            out_copy(head, d).wait_recv()
    for load in loads[5:]:
        load.wait()

    def halo_copy(side):
        start = GRID + (0 if side == 0 else rows - GRID)
        return pltpu.make_async_remote_copy(
            src_ref=maps.at[1, pl.ds(start, GRID)],
            dst_ref=halo.at[side],
            send_sem=halo_send.at[side],
            recv_sem=halo_recv.at[side],
            device_id={"tok": lax.rem(me + (RING - 1 if side == 0 else 1), RING)},
            device_id_type=MESH,
        )

    def spread_columns(plain, at):
        count = plain.shape[0]
        column = lax.broadcasted_iota(jnp.int32, (count, NECK), 0) % GRID
        maps[1, at, :] = plain.astype(bf16)
        maps[0, at, :] = jnp.where(column == 0, 0.0, pltpu.roll(plain, 1, 0)).astype(bf16)
        maps[2, at, :] = jnp.where(column == GRID - 1, 0.0, pltpu.roll(plain, count - 1, 0)).astype(bf16)

    def narrow_tile(i):
        span = pl.ds(pl.multiple_of(i * tile, tile), tile)
        mixed = jnp.concatenate(
            [att[d, :, span] for d in range(RING)], axis=0
        ).T
        block = tok[span, :].astype(f32) + jnp.dot(mixed, wproj[...], preferred_element_type=f32)
        thin = jnp.dot(block.astype(bf16), wn1[...], preferred_element_type=f32)
        thin = norm_rows(thin, g1_ref[...], 1e-06).astype(bf16).astype(f32)
        spread_columns(thin, pl.ds(pl.multiple_of(GRID + i * tile, GRID), tile))

    @pl.loop(0, 2)
    def _(i):
        narrow_tile(i * (tiles - 1))
    halo_copy(0).start()
    halo_copy(1).start()
    @pl.loop(1, tiles - 1)
    def _(i):
        narrow_tile(i)

    def conv_tile(i):
        total = None
        for row_off in range(3):
            at = pl.ds(pl.multiple_of(i * tile + row_off * GRID, GRID), tile)
            for col_off in range(3):
                tap = (row_off * 3 + col_off) * NECK
                part = jnp.dot(maps[col_off, at, :], wn2[tap : tap + NECK, :], preferred_element_type=f32)
                total = part if total is None else total + part
        emb_ref[pl.ds(pl.multiple_of(i * tile, tile), tile), :] = norm_rows(
            total, g2_ref[...], 1e-06
        ).astype(bf16)

    @pl.loop(1, tiles - 1)
    def _(i):
        conv_tile(i)

    halo_copy(0).wait_recv()
    halo_copy(1).wait_recv()
    above = halo[1].astype(f32) * (me > 0).astype(f32)
    below = halo[0].astype(f32) * (me < RING - 1).astype(f32)
    spread_columns(above, pl.ds(0, GRID))
    spread_columns(below, pl.ds(GRID + rows, GRID))

    @pl.loop(0, 2)
    def _(i):
        conv_tile(i * (tiles - 1))

    for kind in range(3):
        for head in range(2):
            for d in range(1, RING):
                qkv_copy(kind, head, d).wait_send()
    for head in range(2):
        for d in range(1, RING):
            out_copy(head, d).wait_send()
    halo_copy(0).wait_send()
    halo_copy(1).wait_send()


def encode(picture, ln_gain, w_qkv, w_proj, w_neck1, gain1, w_neck2, gain2):
    rows, width = picture.shape
    anywhere = pl.BlockSpec(memory_space=pl.ANY)
    local = pl.BlockSpec(memory_space=pltpu.VMEM)
    inner = HEADS * HDIM
    dma = pltpu.SemaphoreType.DMA
    return pl.pallas_call(
        encoder_kernel,
        out_shape=jax.ShapeDtypeStruct((rows, NECK), bf16),
        in_specs=[anywhere, local, anywhere, anywhere, anywhere, local, anywhere, local],
        out_specs=local,
        scratch_shapes=[
            pltpu.VMEM((rows, width), bf16),
            pltpu.VMEM(w_qkv.shape, bf16),
            pltpu.VMEM(w_proj.shape, bf16),
            pltpu.VMEM(w_neck1.shape, bf16),
            pltpu.VMEM(w_neck2.shape, bf16),
            pltpu.VMEM((rows, width), bf16),
            pltpu.VMEM((3 * inner, rows), bf16),
            pltpu.VMEM((3, 2, RING, HDIM, rows), bf16),
            pltpu.VMEM((RING, rows, 128), bf16),
            pltpu.VMEM((2, RING, HDIM, rows), bf16),
            pltpu.VMEM((RING, 2 * HDIM, rows), bf16),
            pltpu.VMEM((3, rows + 2 * GRID, NECK), bf16),
            pltpu.VMEM((2, GRID, NECK), bf16),
            dma((11,)),
            dma((3, 2, RING)),
            dma((3, 2, RING)),
            dma((2, RING)),
            dma((2, RING)),
            dma((2,)),
            dma((2,)),
        ],
        compiler_params=pltpu.CompilerParams(
            collective_id=0, has_side_effects=True, vmem_limit_bytes=60 * 1024 * 1024
        ),
    )(
        picture, ln_gain.reshape(1, -1), w_qkv, w_proj, w_neck1, gain1.reshape(1, -1), w_neck2,
        gain2.reshape(1, -1),
    )


def merged(value, axis, join):
    pieces = jax.tree.map(lambda part: lax.all_gather(part, axis), value)
    head = jax.tree.map(lambda part: part[0], pieces)
    tail = jax.tree.map(lambda part: part[1:], pieces)
    total, _ = lax.scan(lambda total, share: (join(total, share), None), head, tail)
    return total


def layer_norm(tensor, gain_vec, epsilon):
    average = jnp.mean(tensor, axis=-1, keepdims=True)
    centred = tensor - average
    spread = jnp.mean(centred * centred, axis=-1, keepdims=True)
    return centred * lax.rsqrt(spread + epsilon) * gain_vec


def fourier(coords, pe_matrix):
    angles = 2.0 * math.pi * jnp.dot(coords, pe_matrix, precision=highest_precision)
    return jnp.concatenate([jnp.sin(angles), jnp.cos(angles)], axis=-1)


def grid_codes(first_row, grid_rows, pe_matrix):
    row_ids = (first_row + jnp.arange(grid_rows, dtype=jnp.int32)).astype(jnp.float32)
    col_ids = jnp.arange(GRID, dtype=jnp.int32).astype(jnp.float32)
    ycoord = (row_ids + 0.5) / GRID * 2.0 - 1.0
    xcoord = (col_ids + 0.5) / GRID * 2.0 - 1.0
    coords = jnp.stack(
        [
            jnp.broadcast_to(xcoord[None, :], (grid_rows, GRID)),
            jnp.broadcast_to(ycoord[:, None], (grid_rows, GRID)),
        ],
        axis=-1,
    )
    return fourier(coords.reshape(grid_rows * GRID, 2), pe_matrix)


def upscale(embedding, grid_rows, w_up1, up_gain, w_up2):
    first_out = jnp.dot(embedding, w_up1, precision=highest_precision).reshape(
        grid_rows * GRID * 4, UP1
    )
    first_out = jax.nn.gelu(layer_norm(first_out, up_gain, 1e-06), approximate=False)
    second = jax.nn.gelu(jnp.dot(first_out, w_up2, precision=highest_precision), approximate=False)
    second = second.reshape(grid_rows, GRID, 2, 2, 2, 2, UP2)
    second = jnp.transpose(second, (6, 0, 2, 4, 1, 3, 5))
    return second.reshape(UP2, grid_rows * GRID * 16)


def token_side(query_tok, attended, dec_out, dec_gains, w_mlp1, w_mlp2, w_hyper, w_hyper_out):
    first_out = layer_norm(
        query_tok + jnp.dot(attended, dec_out, precision=highest_precision), dec_gains[0], 1e-05
    )
    hidden = jax.nn.relu(jnp.dot(first_out, w_mlp1, precision=highest_precision))
    second = layer_norm(
        first_out + jnp.dot(hidden, w_mlp2, precision=highest_precision), dec_gains[1], 1e-05
    )
    hyper_vec = jax.nn.relu(jnp.dot(second, w_hyper[0], precision=highest_precision))
    hyper_vec = jax.nn.relu(jnp.dot(hyper_vec, w_hyper[1], precision=highest_precision))
    return jnp.dot(hyper_vec, w_hyper_out, precision=highest_precision)


def combine(earlier, later):
    max_a, total_a, mix_a = earlier
    max_b, total_b, mix_b = later
    new_max = jnp.maximum(max_a, max_b)
    scale_a = jnp.exp(max_a - new_max)
    scale_b = jnp.exp(max_b - new_max)
    return (
        new_max,
        total_a * scale_a + total_b * scale_b,
        mix_a * scale_a[:, :, None] + mix_b * scale_b[:, :, None],
    )


def body(
    tokens,
    ln_gain,
    w_qkv,
    w_proj,
    w_neck1,
    neck_gain1,
    w_neck2,
    neck_gain2,
    pe_matrix,
    query_bias,
    dec_qkv,
    dec_out,
    dec_gains,
    w_mlp1,
    w_mlp2,
    w_hyper,
    w_hyper_out,
    w_up1,
    up_gain,
    w_up2,
    req_image,
    points,
):
    picture = tokens[0]
    tok_rows = picture.shape[0]
    grid_rows = tok_rows // GRID
    embedding = encode(
        picture, ln_gain, w_qkv, w_proj, w_neck1, neck_gain1, w_neck2, neck_gain2
    ).astype(jnp.float32)
    positional = grid_codes(lax.axis_index("tok") * grid_rows, grid_rows, pe_matrix)
    head_size = ATTN_DIM // DEC_HEADS
    decoder_scale = 1.0 / math.sqrt(head_size)
    key_projected = jnp.dot(
        embedding + positional, dec_qkv[1], precision=highest_precision
    ).reshape(tok_rows, DEC_HEADS, head_size)
    value_projected = jnp.dot(embedding, dec_qkv[2], precision=highest_precision).reshape(
        tok_rows, DEC_HEADS, head_size
    )
    owners = lax.axis_size("img")
    targets = req_image[:, 0]
    matches = (targets[:, None] == jnp.arange(owners, dtype=jnp.int32)[None, :]).astype(jnp.int32)
    order_no = jnp.sum((jnp.cumsum(matches, axis=0) - matches) * matches, axis=1)
    places = targets * CAP + order_no
    placing = (places[:, None] == jnp.arange(owners * CAP, dtype=jnp.int32)[None, :]).astype(
        jnp.float32
    )
    outgoing = jnp.einsum(
        "sp,sc->pc", placing, points.astype(jnp.float32), precision=highest_precision
    )
    outgoing = outgoing.astype(jnp.int32).reshape(owners, CAP, 2)
    arrived = lax.all_to_all(outgoing, "img", split_axis=0, concat_axis=0, tiled=True)
    number = arrived.shape[1]
    flattened = arrived.reshape(owners * number, 2).astype(jnp.float32)
    query_tok = query_bias + fourier((flattened + 0.5) / IMG_SIDE * 2.0 - 1.0, pe_matrix)
    query_matrix = jnp.dot(query_tok, dec_qkv[0], precision=highest_precision).reshape(
        owners * number, DEC_HEADS, head_size
    )
    attention_scores = (
        jnp.einsum("nex,uex->neu", query_matrix, key_projected, precision=highest_precision)
        * decoder_scale
    )
    maxima = jnp.max(attention_scores, axis=2)
    attention_weights = jnp.exp(attention_scores - maxima[:, :, None])
    totals = jnp.sum(attention_weights, axis=2)
    mixed_values = jnp.einsum(
        "utx,xte->ute", attention_weights, value_projected, precision=highest_precision
    )
    maxima, totals, mixed_values = merged((maxima, totals, mixed_values), "tok", combine)
    cross = (mixed_values / totals[:, :, None]).reshape(owners * number, ATTN_DIM)
    hyper_vec = token_side(
        query_tok, cross, dec_out, dec_gains, w_mlp1, w_mlp2, w_hyper, w_hyper_out
    )
    upscaled = upscale(embedding, grid_rows, w_up1, up_gain, w_up2)
    logits = jnp.dot(hyper_vec, upscaled, precision=highest_precision).astype(bf16)
    logits = logits.reshape(owners, number, -1)
    answer = lax.all_to_all(logits, "img", split_axis=0, concat_axis=0, tiled=True)
    flat_back = answer.reshape(owners * CAP, answer.shape[2])
    result = jnp.take(flat_back, places, axis=0)
    return result.astype(f32)


def solution(mesh):
    placed = (
        P("img", "tok", None),
        P(),
        P(),
        P(),
        P(),
        P(),
        P(),
        P(),
        P(),
        P(),
        P(),
        P(),
        P(),
        P(),
        P(),
        P(),
        P(),
        P(),
        P(),
        P(),
        P("img", None),
        P("img", None),
    )
    return jax.shard_map(
        body, mesh=mesh, in_specs=placed, out_specs=P("img", "tok"), check_vma=False
    )
```

```python
import math

import jax
import jax.numpy as jnp
from jax import lax
from jax.experimental import pallas as pl
from jax.experimental.pallas import tpu as pltpu
from jax.sharding import PartitionSpec as P

HEADS = 8
HDIM = 80
GRID = 64
NECK = 256
ATTN_DIM = 128
DEC_HEADS = 8
UP1 = 64
UP2 = 32
IMG_SIDE = 1024
CAP = 4
RING = 4
MESH = pl.DeviceIdType.MESH
bf16 = jnp.bfloat16
f32 = jnp.float32
LOG2E = math.log2(math.e)
highest_precision = lax.Precision.HIGHEST


def norm_rows(x, gain, eps):
    centred = x - jnp.mean(x, axis=-1, keepdims=True)
    spread = jnp.mean(centred * centred, axis=-1, keepdims=True)
    return centred * lax.rsqrt(spread + eps) * gain


def iota(shape, axis):
    return lax.broadcasted_iota(jnp.int32, shape, axis)


def dot(a, b):
    return jnp.dot(a, b, preferred_element_type=f32)


def exact_dot(a, b):
    return jnp.dot(a, b, preferred_element_type=f32, precision=highest_precision)


def gelu(x):
    return 0.5 * x * (1.0 + lax.erf(x * math.sqrt(0.5)))


def order_numbers(targets, owners):
    count = targets.shape[0]
    match = (iota((count, owners), 1) == targets).astype(f32)
    earlier = (iota((count, count), 0) > iota((count, count), 1)).astype(f32)
    seen = dot(earlier.astype(bf16), match.astype(bf16))
    return jnp.sum(seen * match, axis=1, keepdims=True).astype(jnp.int32)


def split(x):
    high = x.astype(bf16)
    return high, (x - high.astype(f32)).astype(bf16)


def decoder_kernel(
    req_ref, points_ref, emb_ref, pe_ref, bias_ref, dec_qkv_ref, dec_out_ref, dec_gains_ref,
    mlp1_hbm, mlp2_hbm, hyper_hbm, hyper_out_ref, up1_ref, up_gain_ref, up2_ref,
    recv_hbm,
    outgoing, arrived, mlp1, mlp2, hyper, keys, values, mixed, level, got_mixed, got_level, ups, ready,
    load_sem, point_send, point_recv, stat_send, stat_recv, own_sem, mask_send, mask_recv,
):
    img = lax.axis_index("img")
    tok = lax.axis_index("tok")
    owners = recv_hbm.shape[0]
    slots = owners * CAP
    rows = emb_ref.shape[0]
    width = ATTN_DIM // DEC_HEADS

    loads = [
        pltpu.make_async_copy(a, b, load_sem.at[i])
        for i, (a, b) in enumerate(((mlp1_hbm, mlp1), (mlp2_hbm, mlp2), (hyper_hbm, hyper)))
    ]
    for load in loads:
        load.start()

    def partner(k, sign):
        dx, dy, dc = k // 8, (k // 2) % 4, k % 2
        x, y, core = img // 8, (img // 2) % 4, img % 2
        return (
            lax.rem(x + sign * dx + 4, 4) * 8 + lax.rem(y + sign * dy + 4, 4) * 2 + lax.rem(core + dc, 2)
        )

    barrier = pltpu.get_barrier_semaphore()

    @pl.loop(1, owners)
    def _(k):
        pl.semaphore_signal(barrier, inc=1, device_id={"img": partner(k, 1)}, device_id_type=MESH)

    for d in range(1, RING):
        pl.semaphore_signal(
            barrier, inc=1, device_id={"tok": lax.rem(tok + d, RING)}, device_id_type=MESH
        )

    targets = req_ref[...]
    order_no = order_numbers(targets, owners)
    place = targets * 8 + order_no
    placing = (iota((targets.shape[0], owners * 8), 1) == place).astype(f32).T.astype(bf16)
    lane = iota((targets.shape[0], 128), 1)
    px, py = points_ref[:, 0:1], points_ref[:, 1:2]
    parts = jnp.where(
        lane == 0, px // 32, jnp.where(lane == 1, px % 32, jnp.where(lane == 2, py // 32, jnp.where(lane == 3, py % 32, 0)))
    )
    outgoing[...] = dot(placing, parts.astype(f32).astype(bf16)).reshape(owners, 8, 128)

    pl.semaphore_wait(barrier, owners - 1 + RING - 1)

    def point_copy(k):
        to = partner(k, 1)
        return pltpu.make_async_remote_copy(
            src_ref=outgoing.at[to], dst_ref=arrived.at[img],
            send_sem=point_send.at[k], recv_sem=point_recv.at[k],
            device_id={"img": to}, device_id_type=MESH,
        )

    @pl.loop(1, owners)
    def _(k):
        point_copy(k).start()
    arrived[img] = outgoing[img]

    turn = 2.0 * math.pi
    px_row, py_row = pe_ref[0:1, :], pe_ref[1:2, :]
    grid_rows = rows // GRID
    col_angle = turn * (((iota((GRID, 128), 0).astype(f32) + 0.5) / GRID * 2.0 - 1.0) * px_row)
    row_no = iota((grid_rows, 128), 0) + tok * grid_rows
    row_angle = turn * (((row_no.astype(f32) + 0.5) / GRID * 2.0 - 1.0) * py_row)
    col_sin, col_cos = jnp.sin(col_angle), jnp.cos(col_angle)
    row_sin, row_cos = jnp.sin(row_angle), jnp.cos(row_angle)
    key_w = dec_qkv_ref[1]
    value_w = dec_qkv_ref[2].astype(bf16)
    key_high, key_low = split(key_w)
    for r in range(grid_rows):
        span = pl.ds(r * GRID, GRID)
        rs, rc = row_sin[r : r + 1], row_cos[r : r + 1]
        code = jnp.concatenate(
            [col_sin * rc + col_cos * rs, col_cos * rc - col_sin * rs], axis=1
        )
        cell = emb_ref[span, :]
        high, low = split(cell + code)
        projected = dot(high, key_high) + (dot(high, key_low) + dot(low, key_high))
        k_high, k_low = split(projected)
        keys[span, 0:128] = k_high
        keys[span, 128:256] = k_low
        values[span, :] = dot(cell.astype(bf16), value_w).astype(bf16)

    @pl.loop(1, owners)
    def _(k):
        point_copy(k).wait_recv()

    row = iota((slots, owners * 8), 0)
    pick = (iota((slots, owners * 8), 1) == (row // CAP) * 8 + row % CAP).astype(bf16)
    picked = dot(pick, arrived[...].reshape(owners * 8, 128).astype(bf16))
    where_x = picked[:, 0:1] * 32.0 + picked[:, 1:2]
    where_y = picked[:, 2:3] * 32.0 + picked[:, 3:4]
    angle = turn * (
        ((where_x + 0.5) / IMG_SIDE * 2.0 - 1.0) * px_row + ((where_y + 0.5) / IMG_SIDE * 2.0 - 1.0) * py_row
    )
    query_tok = bias_ref[...] + jnp.concatenate([jnp.sin(angle), jnp.cos(angle)], axis=1)
    query = exact_dot(query_tok, dec_qkv_ref[0]) * (LOG2E / math.sqrt(width))
    head_of = iota((slots, 128), 1) // width
    mix = jnp.zeros((slots, 128), f32)
    lev = jnp.zeros((slots, 128), f32)
    contract = (((1,), (1,)), ((), ()))
    for e in range(DEC_HEADS):
        q_high, q_low = split(jnp.where(head_of == e, query, 0.0))
        scores = lax.dot_general(
            jnp.concatenate([q_high, q_high], axis=1), keys[...], contract, preferred_element_type=f32
        ) + lax.dot_general(q_low, keys[:, 0:128], contract, preferred_element_type=f32)
        top = jnp.max(scores, axis=1, keepdims=True)
        weights = jnp.exp2(scores - top)
        total = jnp.sum(weights, axis=1, keepdims=True)
        part = dot(weights.astype(bf16), values[...]) / total
        mix = jnp.where(head_of == e, part, mix)
        lev = jnp.where(head_of == e, top + jnp.log(total) * LOG2E, lev)
    mixed[...] = mix.astype(bf16)
    level[...] = lev

    def stat_copy(kind, d):
        src, dst = ((mixed, got_mixed), (level, got_level))[kind]
        return pltpu.make_async_remote_copy(
            src_ref=src, dst_ref=dst.at[d],
            send_sem=stat_send.at[kind, d], recv_sem=stat_recv.at[kind, d],
            device_id={"tok": lax.rem(tok + d, RING)}, device_id_type=MESH,
        )

    for d in (2, 1, 3):
        stat_copy(0, d).start()
        stat_copy(1, d).start()

    gain_col = jnp.sum(
        jnp.where(iota((UP1, UP1), 0) == iota((UP1, UP1), 1), up_gain_ref[...], 0.0), axis=1, keepdims=True
    )
    first_w = up1_ref[...].T.astype(bf16)
    second_w = up2_ref[...].T.astype(bf16)
    lanes = 256

    @pl.loop(0, rows // lanes)
    def _(i):
        span = pl.ds(pl.multiple_of(i * lanes, lanes), lanes)
        wide = lax.dot_general(
            first_w, emb_ref[span, :].astype(bf16), contract, preferred_element_type=f32
        )
        for g in range(4):
            part = wide[g * UP1 : (g + 1) * UP1]
            centred = part - jnp.mean(part, axis=0, keepdims=True)
            spread = jnp.mean(centred * centred, axis=0, keepdims=True)
            first = gelu(centred * lax.rsqrt(spread + 1e-06) * gain_col)
            ups[g, :, span] = gelu(dot(second_w, first.astype(bf16))).astype(bf16)

    for load in loads:
        load.wait()
    for d in range(1, RING):
        stat_copy(0, d).wait_recv()
        stat_copy(1, d).wait_recv()
    levels = [lev] + [got_level[d] for d in range(1, RING)]
    parts = [mixed[...].astype(f32)] + [got_mixed[d].astype(f32) for d in range(1, RING)]
    peak = jnp.maximum(jnp.maximum(levels[0], levels[1]), jnp.maximum(levels[2], levels[3]))
    shares = [jnp.exp2(item - peak) for item in levels]
    cross = sum(s * p for s, p in zip(shares, parts)) / sum(shares)

    first_out = norm_rows(
        query_tok + dot(cross.astype(bf16), dec_out_ref[...].astype(bf16)), dec_gains_ref[0:1, :], 1e-05
    )
    hidden = jnp.maximum(dot(first_out.astype(bf16), mlp1[...].astype(bf16)), 0.0)
    second = norm_rows(
        first_out + dot(hidden.astype(bf16), mlp2[...].astype(bf16)), dec_gains_ref[1:2, :], 1e-05
    )
    vec = jnp.maximum(dot(second.astype(bf16), hyper[0].astype(bf16)), 0.0)
    vec = jnp.maximum(dot(vec.astype(bf16), hyper[1].astype(bf16)), 0.0)
    last = hyper_out_ref[...]
    vec = dot(vec.astype(bf16), jnp.concatenate([last] * 4, axis=1).astype(bf16)).astype(bf16)
    big = owners * 16
    row = iota((big, slots), 0)
    repeat = (iota((big, slots), 1) == (row // 16) * CAP + row % CAP).astype(bf16)
    row = iota((big, 128), 0)
    stacked = jnp.where((row // CAP) % 4 == iota((big, 128), 1) // UP2, dot(repeat, vec), 0.0).astype(bf16)

    def mask_copy(g, k):
        to = partner(k, 1)
        return pltpu.make_async_remote_copy(
            src_ref=ready.at[g, to], dst_ref=recv_hbm.at[img, g],
            send_sem=mask_send.at[g, k], recv_sem=mask_recv.at[g, k],
            device_id={"img": to}, device_id_type=MESH,
        )

    def own_copy(g):
        return pltpu.make_async_copy(ready.at[g, img], recv_hbm.at[img, g], own_sem.at[g])

    for g in range(4):
        ready[g] = dot(stacked, ups[g]).astype(bf16).reshape(owners, 16, rows)

        @pl.loop(1, owners)
        def _(k):
            mask_copy(g, lax.rem(k * 13, owners)).start()
        own_copy(g).start()

    @pl.loop(1, owners)
    def _(k):
        point_copy(k).wait_send()
    for d in range(1, RING):
        stat_copy(0, d).wait_send()
        stat_copy(1, d).wait_send()
    for g in range(4):
        own_copy(g).wait()

        @pl.loop(1, owners)
        def _(k):
            mask_copy(g, k).wait_recv()
            mask_copy(g, k).wait_send()


def decode(
    req_image, points, embedding, pe_matrix, query_bias, dec_qkv, dec_out, dec_gains, w_mlp1, w_mlp2,
    w_hyper, w_hyper_out, w_up1, up_gain, w_up2, owners,
):
    anywhere = pl.BlockSpec(memory_space=pl.ANY)
    local = pl.BlockSpec(memory_space=pltpu.VMEM)
    rows = embedding.shape[0]
    slots = owners * CAP
    dma = pltpu.SemaphoreType.DMA
    return pl.pallas_call(
        decoder_kernel,
        out_shape=jax.ShapeDtypeStruct((owners, 4, 16, rows), bf16),
        in_specs=[local] * 8 + [anywhere] * 3 + [local] * 4,
        out_specs=anywhere,
        scratch_shapes=[
            pltpu.VMEM((owners, 8, 128), f32),
            pltpu.VMEM((owners, 8, 128), f32),
            pltpu.VMEM(w_mlp1.shape, f32),
            pltpu.VMEM(w_mlp2.shape, f32),
            pltpu.VMEM(w_hyper.shape, f32),
            pltpu.VMEM((rows, 256), bf16),
            pltpu.VMEM((rows, 128), bf16),
            pltpu.VMEM((slots, 128), bf16),
            pltpu.VMEM((slots, 128), f32),
            pltpu.VMEM((RING, slots, 128), bf16),
            pltpu.VMEM((RING, slots, 128), f32),
            pltpu.VMEM((4, 128, rows), bf16),
            pltpu.VMEM((4, owners, 16, rows), bf16),
            dma((3,)),
            dma((owners,)),
            dma((owners,)),
            dma((2, RING)),
            dma((2, RING)),
            dma((4,)),
            dma((4, owners)),
            dma((4, owners)),
        ],
        compiler_params=pltpu.CompilerParams(
            collective_id=1, has_side_effects=True, vmem_limit_bytes=60 * 1024 * 1024
        ),
    )(
        req_image, points, embedding, pe_matrix, query_bias.reshape(1, -1), dec_qkv, dec_out, dec_gains,
        w_mlp1, w_mlp2, w_hyper, w_hyper_out, w_up1, up_gain.reshape(1, -1), w_up2,
    )


def select_kernel(req_ref, recv_ref, out_ref, chooser, mover):
    owners = recv_ref.shape[0]
    slots = req_ref.shape[0]

    @pl.when(pl.program_id(0) == 0)
    def _():
        targets = req_ref[...]
        place = targets * 16 + order_numbers(targets, owners)
        for k in range(4):
            chooser[k * slots : (k + 1) * slots, :] = (
                iota((slots, owners * 16), 1) == place + k * CAP
            ).astype(bf16)
        row, col = iota((512, 512), 0), iota((512, 512), 1)
        inside = row % 128
        mover[...] = (col == (inside // GRID) * 256 + (inside % GRID) * 4 + row // 128).astype(bf16)

    chosen = [
        dot(chooser[...], recv_ref[:, g].reshape(owners * 16, 128)).astype(bf16) for g in range(4)
    ]
    for dr in range(2):
        for er in range(2):
            side = jnp.concatenate(
                [
                    chosen[dr * 2 + dc][(er * 2 + ec) * slots : (er * 2 + ec + 1) * slots]
                    for dc in range(2)
                    for ec in range(2)
                ],
                axis=1,
            )
            lines = dot(side, mover[...])
            for r in range(2):
                line = (r * 4 + dr * 2 + er) * 256
                out_ref[:, line : line + 256] = lines[:, r * 256 : (r + 1) * 256]


def select(req_image, received):
    owners, _, _, rows = received.shape
    slots = req_image.shape[0]
    steps = rows // 128
    return pl.pallas_call(
        select_kernel,
        out_shape=jax.ShapeDtypeStruct((slots, rows * 16), f32),
        grid=(steps,),
        in_specs=[
            pl.BlockSpec((slots, 1), lambda i: (0, 0)),
            pl.BlockSpec((owners, 4, 16, 128), lambda i: (0, 0, 0, i)),
        ],
        out_specs=pl.BlockSpec((slots, 2048), lambda i: (0, i)),
        scratch_shapes=[
            pltpu.VMEM((4 * slots, owners * 16), bf16),
            pltpu.VMEM((512, 512), bf16),
        ],
        compiler_params=pltpu.CompilerParams(vmem_limit_bytes=32 * 1024 * 1024),
    )(req_image, received)


def encoder_kernel(
    tok_hbm, gain_ref, wqkv_hbm, wproj_hbm, wn1_hbm, g1_ref, wn2_hbm, g2_ref,
    emb_ref,
    tok, wqkv, wproj, wn1, wn2, normed, loc, got, vrows, outs, att, maps,
    halo, load_sem, qkv_send, qkv_recv, out_send, out_recv, halo_send, halo_recv,
):
    me = lax.axis_index("tok")
    rows = tok.shape[0]
    two = 2 * HDIM
    inner = HEADS * HDIM
    tile = 256
    tiles = rows // tile
    qblock = 512

    loads = [
        pltpu.make_async_copy(tok_hbm.at[pl.ds(i * tile, tile)], tok.at[pl.ds(i * tile, tile)], load_sem.at[i])
        for i in range(tiles)
    ]
    loads.append(pltpu.make_async_copy(wqkv_hbm, wqkv, load_sem.at[4]))
    loads.append(pltpu.make_async_copy(wn1_hbm, wn1, load_sem.at[5]))
    loads.append(pltpu.make_async_copy(wn2_hbm, wn2, load_sem.at[6]))
    for d in range(RING):
        owner = lax.rem(me + d, RING)
        loads.append(
            pltpu.make_async_copy(
                wproj_hbm.at[pl.ds(pl.multiple_of(owner * two, 32), two)],
                wproj.at[pl.ds(d * two, two)],
                load_sem.at[7 + d],
            )
        )
    for load in loads:
        load.start()

    barrier = pltpu.get_barrier_semaphore()
    for d in range(1, RING):
        pl.semaphore_signal(
            barrier, inc=1, device_id={"tok": lax.rem(me + d, RING)}, device_id_type=MESH
        )
    pl.semaphore_wait(barrier, RING - 1)

    for i in range(tiles):
        loads[i].wait()
        span = pl.ds(i * tile, tile)
        normed[span, :] = norm_rows(tok[span, :].astype(f32), gain_ref[...], 1e-06).astype(bf16)
    loads[4].wait()

    scale = math.log2(math.e) / math.sqrt(HDIM)

    def qkv_copy(kind, head, d):
        owner = lax.rem(me + d, RING)
        first = pl.multiple_of(kind * inner + owner * two + head * HDIM, 16)
        return pltpu.make_async_remote_copy(
            src_ref=loc.at[pl.ds(first, HDIM)],
            dst_ref=got.at[kind, head, d],
            send_sem=qkv_send.at[kind, head, d],
            recv_sem=qkv_recv.at[kind, head, d],
            device_id={"tok": owner},
            device_id_type=MESH,
        )

    def project(kind):
        @pl.loop(0, tiles)
        def _(i):
            span = pl.ds(pl.multiple_of(i * tile, tile), tile)
            part = jnp.dot(
                normed[span, :], wqkv[:, kind * inner : (kind + 1) * inner], preferred_element_type=f32
            )
            if kind == 0:
                part = part * scale
            loc[kind * inner : (kind + 1) * inner, span] = part.astype(bf16).T

    for kind in (1, 2, 0):
        project(kind)
        for d in (1, 3, 2):
            qkv_copy(kind, 0, d).start()
    for kind in (1, 2, 0):
        for d in (1, 3, 2):
            qkv_copy(kind, 1, d).start()
    for kind in range(3):
        for head in range(2):
            first = pl.multiple_of(kind * inner + me * two + head * HDIM, 16)
            got[kind, head, 0] = loc[pl.ds(first, HDIM), :]

    def out_copy(head, d):
        target = lax.rem(me - d + RING, RING)
        return pltpu.make_async_remote_copy(
            src_ref=outs.at[head, d],
            dst_ref=att.at[d, pl.ds(pl.multiple_of(head * HDIM, 16), HDIM)],
            send_sem=out_send.at[head, d],
            recv_sem=out_recv.at[head, d],
            device_id={"tok": target},
            device_id_type=MESH,
        )

    filler = (lax.broadcasted_iota(jnp.int32, (48, rows), 0) == 0).astype(bf16)
    halves = rows // qblock

    @pl.loop(0, 2)
    def _(head):
        for d in range(1, RING):
            qkv_copy(1, head, d).wait_recv()
            qkv_copy(2, head, d).wait_recv()
        for d in range(RING):
            vrows[d] = jnp.concatenate([got[2, head, d], filler], axis=0).T

        @pl.loop(0, RING)
        def _(turn):
            slot = lax.rem(turn + head, RING)

            @pl.when(slot > 0)
            def _():
                qkv_copy(0, head, slot).wait_recv()

            @pl.loop(0, halves)
            def _(half):
                span = pl.ds(pl.multiple_of(half * qblock, qblock), qblock)
                query = got[0, head, slot, :, span].T

                def scores(d):
                    return jnp.dot(query, got[1, head, d], preferred_element_type=f32)

                now = scores(0)
                top = None
                for d in range(RING):
                    ahead = scores(d + 1) if d + 1 < RING else None
                    here = jnp.max(now, axis=1, keepdims=True)
                    fresh = here if top is None else jnp.maximum(top, here)
                    weights = jnp.exp2(now - fresh).astype(bf16)
                    part = jnp.dot(weights, vrows[d], preferred_element_type=f32)
                    total = part if top is None else total * jnp.exp2(top - fresh) + part
                    top, now = fresh, ahead
                final = (total * (1.0 / total[:, HDIM : HDIM + 1])).astype(bf16).T[:HDIM]
                outs[head, slot, :, span] = final

            @pl.when(slot > 0)
            def _():
                out_copy(head, slot).start()

            @pl.when(slot == 0)
            def _():
                att[0, pl.ds(pl.multiple_of(head * HDIM, 16), HDIM), :] = outs[head, 0]

    for d in range(1, RING):
        for head in range(2):
            out_copy(head, d).wait_recv()
    for load in loads[5:]:
        load.wait()

    def halo_copy(side):
        start = GRID + (0 if side == 0 else rows - GRID)
        return pltpu.make_async_remote_copy(
            src_ref=maps.at[1, pl.ds(start, GRID)],
            dst_ref=halo.at[side],
            send_sem=halo_send.at[side],
            recv_sem=halo_recv.at[side],
            device_id={"tok": lax.rem(me + (RING - 1 if side == 0 else 1), RING)},
            device_id_type=MESH,
        )

    def spread_columns(plain, at):
        count = plain.shape[0]
        column = lax.broadcasted_iota(jnp.int32, (count, NECK), 0) % GRID
        maps[1, at, :] = plain.astype(bf16)
        maps[0, at, :] = jnp.where(column == 0, 0.0, pltpu.roll(plain, 1, 0)).astype(bf16)
        maps[2, at, :] = jnp.where(column == GRID - 1, 0.0, pltpu.roll(plain, count - 1, 0)).astype(bf16)

    def narrow_tile(i):
        span = pl.ds(pl.multiple_of(i * tile, tile), tile)
        mixed = jnp.concatenate(
            [att[d, :, span] for d in range(RING)], axis=0
        ).T
        block = tok[span, :].astype(f32) + jnp.dot(mixed, wproj[...], preferred_element_type=f32)
        thin = jnp.dot(block.astype(bf16), wn1[...], preferred_element_type=f32)
        thin = norm_rows(thin, g1_ref[...], 1e-06).astype(bf16).astype(f32)
        spread_columns(thin, pl.ds(pl.multiple_of(GRID + i * tile, GRID), tile))

    @pl.loop(0, 2)
    def _(i):
        narrow_tile(i * (tiles - 1))
    halo_copy(0).start()
    halo_copy(1).start()
    @pl.loop(1, tiles - 1)
    def _(i):
        narrow_tile(i)

    def conv_tile(i):
        total = None
        for row_off in range(3):
            at = pl.ds(pl.multiple_of(i * tile + row_off * GRID, GRID), tile)
            for col_off in range(3):
                tap = (row_off * 3 + col_off) * NECK
                part = jnp.dot(maps[col_off, at, :], wn2[tap : tap + NECK, :], preferred_element_type=f32)
                total = part if total is None else total + part
        emb_ref[pl.ds(pl.multiple_of(i * tile, tile), tile), :] = norm_rows(
            total, g2_ref[...], 1e-06
        )

    @pl.loop(1, tiles - 1)
    def _(i):
        conv_tile(i)

    halo_copy(0).wait_recv()
    halo_copy(1).wait_recv()
    above = halo[1].astype(f32) * (me > 0).astype(f32)
    below = halo[0].astype(f32) * (me < RING - 1).astype(f32)
    spread_columns(above, pl.ds(0, GRID))
    spread_columns(below, pl.ds(GRID + rows, GRID))

    @pl.loop(0, 2)
    def _(i):
        conv_tile(i * (tiles - 1))

    for kind in range(3):
        for head in range(2):
            for d in range(1, RING):
                qkv_copy(kind, head, d).wait_send()
    for head in range(2):
        for d in range(1, RING):
            out_copy(head, d).wait_send()
    halo_copy(0).wait_send()
    halo_copy(1).wait_send()


def encode(picture, ln_gain, w_qkv, w_proj, w_neck1, gain1, w_neck2, gain2):
    rows, width = picture.shape
    anywhere = pl.BlockSpec(memory_space=pl.ANY)
    local = pl.BlockSpec(memory_space=pltpu.VMEM)
    inner = HEADS * HDIM
    dma = pltpu.SemaphoreType.DMA
    return pl.pallas_call(
        encoder_kernel,
        out_shape=jax.ShapeDtypeStruct((rows, NECK), f32),
        in_specs=[anywhere, local, anywhere, anywhere, anywhere, local, anywhere, local],
        out_specs=local,
        scratch_shapes=[
            pltpu.VMEM((rows, width), bf16),
            pltpu.VMEM(w_qkv.shape, bf16),
            pltpu.VMEM(w_proj.shape, bf16),
            pltpu.VMEM(w_neck1.shape, bf16),
            pltpu.VMEM(w_neck2.shape, bf16),
            pltpu.VMEM((rows, width), bf16),
            pltpu.VMEM((3 * inner, rows), bf16),
            pltpu.VMEM((3, 2, RING, HDIM, rows), bf16),
            pltpu.VMEM((RING, rows, 128), bf16),
            pltpu.VMEM((2, RING, HDIM, rows), bf16),
            pltpu.VMEM((RING, 2 * HDIM, rows), bf16),
            pltpu.VMEM((3, rows + 2 * GRID, NECK), bf16),
            pltpu.VMEM((2, GRID, NECK), bf16),
            dma((11,)),
            dma((3, 2, RING)),
            dma((3, 2, RING)),
            dma((2, RING)),
            dma((2, RING)),
            dma((2,)),
            dma((2,)),
        ],
        compiler_params=pltpu.CompilerParams(
            collective_id=0, has_side_effects=True, vmem_limit_bytes=60 * 1024 * 1024
        ),
    )(
        picture, ln_gain.reshape(1, -1), w_qkv, w_proj, w_neck1, gain1.reshape(1, -1), w_neck2,
        gain2.reshape(1, -1),
    )


def body(
    tokens,
    ln_gain,
    w_qkv,
    w_proj,
    w_neck1,
    neck_gain1,
    w_neck2,
    neck_gain2,
    pe_matrix,
    query_bias,
    dec_qkv,
    dec_out,
    dec_gains,
    w_mlp1,
    w_mlp2,
    w_hyper,
    w_hyper_out,
    w_up1,
    up_gain,
    w_up2,
    req_image,
    points,
):
    embedding = encode(
        tokens[0], ln_gain, w_qkv, w_proj, w_neck1, neck_gain1, w_neck2, neck_gain2
    )
    received = decode(
        req_image, points, embedding, pe_matrix, query_bias, dec_qkv, dec_out, dec_gains, w_mlp1,
        w_mlp2, w_hyper, w_hyper_out, w_up1, up_gain, w_up2, lax.axis_size("img"),
    )
    return select(req_image, received)


def solution(mesh):
    placed = (
        P("img", "tok", None),
        P(),
        P(),
        P(),
        P(),
        P(),
        P(),
        P(),
        P(),
        P(),
        P(),
        P(),
        P(),
        P(),
        P(),
        P(),
        P(),
        P(),
        P(),
        P(),
        P("img", None),
        P("img", None),
    )
    return jax.shard_map(
        body, mesh=mesh, in_specs=placed, out_specs=P("img", "tok"), check_vma=False
    )
```

```python
import math

import jax
import jax.numpy as jnp
from jax import lax
from jax.experimental import pallas as pl
from jax.experimental.pallas import tpu as pltpu
from jax.sharding import PartitionSpec as P

HEADS = 8
HDIM = 80
GRID = 64
NECK = 256
ATTN_DIM = 128
DEC_HEADS = 8
UP1 = 64
UP2 = 32
IMG_SIDE = 1024
CAP = 4
RING = 4
MESH = pl.DeviceIdType.MESH
bf16 = jnp.bfloat16
f32 = jnp.float32
LOG2E = math.log2(math.e)
highest_precision = lax.Precision.HIGHEST


def norm_rows(x, gain, eps):
    centred = x - jnp.mean(x, axis=-1, keepdims=True)
    spread = jnp.mean(centred * centred, axis=-1, keepdims=True)
    return centred * lax.rsqrt(spread + eps) * gain


def iota(shape, axis):
    return lax.broadcasted_iota(jnp.int32, shape, axis)


def dot(a, b):
    return jnp.dot(a, b, preferred_element_type=f32)


def exact_dot(a, b):
    return jnp.dot(a, b, preferred_element_type=f32, precision=highest_precision)


def gelu(x):
    return 0.5 * x * (1.0 + lax.erf(x * math.sqrt(0.5)))


def request_places(targets, owners):
    count = targets.shape[1]
    match = (iota((owners, count), 0) == targets).astype(f32)
    earlier = (iota((count, count), 0) < iota((count, count), 1)).astype(bf16)
    seen = dot(match.astype(bf16), earlier)
    return targets, jnp.sum(seen * match, axis=0, keepdims=True).astype(jnp.int32)


def partner(img, k):
    dx, dy, dc = k // 8, (k // 2) % 4, k % 2
    x, y, core = img // 8, (img // 2) % 4, img % 2
    return lax.rem(x + dx, 4) * 8 + lax.rem(y + dy, 4) * 2 + lax.rem(core + dc, 2)


def split(x):
    high = x.astype(bf16)
    return high, (x - high.astype(f32)).astype(bf16)


def trunk_kernel(
    tok_hbm, gain_ref, wqkv_hbm, wproj_hbm, wn1_hbm, g1_ref, wn2_hbm, g2_ref,
    req_ref, points_ref, pe_ref, bias_ref, dec_qkv_ref, dec_out_ref, dec_gains_ref,
    mlp1_hbm, mlp2_hbm, hyper_hbm, hyper_out_ref, up1_ref, up_gain_ref, up2_ref,
    chosen_ref, mover_ref,
    tok, wqkv, wproj, wn1, wn2, normed, loc, got, vrows, outs, att, maps, halo,
    load_sem, qkv_send, qkv_recv, out_send, out_recv, halo_send, halo_recv,
    emb_ref, outgoing, arrived, mlp1, mlp2, hyper, keys, values, mixed, level, got_mixed, got_level, ups,
    ready, received, chooser,
    late_sem, point_send, point_recv, stat_send, stat_recv, mask_send, mask_recv,
):
    me = lax.axis_index("tok")
    rows = tok.shape[0]
    two = 2 * HDIM
    slots = received.shape[1] * CAP
    contract = (((1,), (1,)), ((), ()))
    inner = HEADS * HDIM
    tile = 256
    tiles = rows // tile
    qblock = 512

    loads = [
        pltpu.make_async_copy(tok_hbm.at[pl.ds(i * tile, tile)], tok.at[pl.ds(i * tile, tile)], load_sem.at[i])
        for i in range(tiles)
    ]
    loads.append(pltpu.make_async_copy(wqkv_hbm, wqkv, load_sem.at[4]))
    loads.append(pltpu.make_async_copy(wn1_hbm, wn1, load_sem.at[5]))
    loads.append(pltpu.make_async_copy(wn2_hbm, wn2, load_sem.at[6]))
    for d in range(RING):
        owner = lax.rem(me + d, RING)
        loads.append(
            pltpu.make_async_copy(
                wproj_hbm.at[pl.ds(pl.multiple_of(owner * two, 32), two)],
                wproj.at[pl.ds(d * two, two)],
                load_sem.at[7 + d],
            )
        )
    late = [
        pltpu.make_async_copy(a, b, late_sem.at[i])
        for i, (a, b) in enumerate(((mlp1_hbm, mlp1), (mlp2_hbm, mlp2), (hyper_hbm, hyper)))
    ]
    for load in loads + late:
        load.start()

    img = lax.axis_index("img")
    owners = received.shape[1]
    barrier = pltpu.get_barrier_semaphore()
    for d in range(1, RING):
        pl.semaphore_signal(
            barrier, inc=1, device_id={"tok": lax.rem(me + d, RING)}, device_id_type=MESH
        )

    @pl.loop(1, owners)
    def _(k):
        pl.semaphore_signal(barrier, inc=1, device_id={"img": partner(img, k)}, device_id_type=MESH)

    for i in range(tiles):
        loads[i].wait()
        span = pl.ds(i * tile, tile)
        normed[span, :] = norm_rows(tok[span, :].astype(f32), gain_ref[...], 1e-06).astype(bf16)
    loads[4].wait()

    scale = math.log2(math.e) / math.sqrt(HDIM)

    def qkv_copy(kind, head, d):
        owner = lax.rem(me + d, RING)
        first = pl.multiple_of(kind * inner + owner * two + head * HDIM, 16)
        return pltpu.make_async_remote_copy(
            src_ref=loc.at[pl.ds(first, HDIM)],
            dst_ref=got.at[kind, head, d],
            send_sem=qkv_send.at[kind, head, d],
            recv_sem=qkv_recv.at[kind, head, d],
            device_id={"tok": owner},
            device_id_type=MESH,
        )

    def project(kind):
        @pl.loop(0, tiles)
        def _(i):
            span = pl.ds(pl.multiple_of(i * tile, tile), tile)
            part = jnp.dot(
                normed[span, :], wqkv[:, kind * inner : (kind + 1) * inner], preferred_element_type=f32
            )
            if kind == 0:
                part = part * scale
            loc[kind * inner : (kind + 1) * inner, span] = part.astype(bf16).T

    for kind in (1, 2, 0):
        project(kind)
        if kind == 1:
            pl.semaphore_wait(barrier, owners - 1 + RING - 1)
        for d in (1, 3, 2):
            qkv_copy(kind, 0, d).start()
    for kind in (1, 2, 0):
        for d in (1, 3, 2):
            qkv_copy(kind, 1, d).start()
    place = request_places(req_ref[...], owners)
    placing = (iota((owners * 8, slots // 2), 0) == place[0] * 8 + place[1]).astype(bf16)
    line = iota((128, slots // 2), 0)
    across, down = points_ref[0:1, :], points_ref[1:2, :]
    parts = jnp.where(
        line == 0,
        across // 32,
        jnp.where(line == 1, across % 32, jnp.where(line == 2, down // 32, jnp.where(line == 3, down % 32, 0))),
    )
    outgoing[...] = lax.dot_general(
        placing, parts.astype(f32).astype(bf16), contract, preferred_element_type=f32
    ).reshape(owners, 8, 128)

    def point_copy(k):
        to = partner(img, k)
        return pltpu.make_async_remote_copy(
            src_ref=outgoing.at[to], dst_ref=arrived.at[img],
            send_sem=point_send.at[k], recv_sem=point_recv.at[k],
            device_id={"img": to}, device_id_type=MESH,
        )

    for kind in range(3):
        for head in range(2):
            first = pl.multiple_of(kind * inner + me * two + head * HDIM, 16)
            got[kind, head, 0] = loc[pl.ds(first, HDIM), :]

    @pl.loop(1, owners)
    def _(k):
        point_copy(k).start()
    arrived[img] = outgoing[img]

    def out_copy(head, d):
        target = lax.rem(me - d + RING, RING)
        return pltpu.make_async_remote_copy(
            src_ref=outs.at[head, d],
            dst_ref=att.at[d, pl.ds(pl.multiple_of(head * HDIM, 16), HDIM)],
            send_sem=out_send.at[head, d],
            recv_sem=out_recv.at[head, d],
            device_id={"tok": target},
            device_id_type=MESH,
        )

    filler = (lax.broadcasted_iota(jnp.int32, (48, rows), 0) == 0).astype(bf16)
    halves = rows // qblock

    @pl.loop(0, 2)
    def _(head):
        for d in range(1, RING):
            qkv_copy(1, head, d).wait_recv()
            qkv_copy(2, head, d).wait_recv()
        for d in range(RING):
            vrows[d] = jnp.concatenate([got[2, head, d], filler], axis=0).T

        @pl.loop(0, RING)
        def _(turn):
            slot = lax.rem(turn + head, RING)

            @pl.when(slot > 0)
            def _():
                qkv_copy(0, head, slot).wait_recv()

            @pl.loop(0, halves)
            def _(half):
                span = pl.ds(pl.multiple_of(half * qblock, qblock), qblock)
                query = got[0, head, slot, :, span].T

                def scores(d):
                    return jnp.dot(query, got[1, head, d], preferred_element_type=f32)

                now = scores(0)
                top = None
                for d in range(RING):
                    ahead = scores(d + 1) if d + 1 < RING else None
                    here = jnp.max(now, axis=1, keepdims=True)
                    fresh = here if top is None else jnp.maximum(top, here)
                    weights = jnp.exp2(now - fresh).astype(bf16)
                    part = jnp.dot(weights, vrows[d], preferred_element_type=f32)
                    total = part if top is None else total * jnp.exp2(top - fresh) + part
                    top, now = fresh, ahead
                final = (total * (1.0 / total[:, HDIM : HDIM + 1])).astype(bf16).T[:HDIM]
                outs[head, slot, :, span] = final

            @pl.when(slot > 0)
            def _():
                out_copy(head, slot).start()

            @pl.when(slot == 0)
            def _():
                att[0, pl.ds(pl.multiple_of(head * HDIM, 16), HDIM), :] = outs[head, 0]

    for d in range(1, RING):
        for head in range(2):
            out_copy(head, d).wait_recv()
    for load in loads[5:]:
        load.wait()

    def halo_copy(side):
        start = GRID + (0 if side == 0 else rows - GRID)
        return pltpu.make_async_remote_copy(
            src_ref=maps.at[1, pl.ds(start, GRID)],
            dst_ref=halo.at[side],
            send_sem=halo_send.at[side],
            recv_sem=halo_recv.at[side],
            device_id={"tok": lax.rem(me + (RING - 1 if side == 0 else 1), RING)},
            device_id_type=MESH,
        )

    def spread_columns(plain, at):
        count = plain.shape[0]
        column = lax.broadcasted_iota(jnp.int32, (count, NECK), 0) % GRID
        maps[1, at, :] = plain.astype(bf16)
        maps[0, at, :] = jnp.where(column == 0, 0.0, pltpu.roll(plain, 1, 0)).astype(bf16)
        maps[2, at, :] = jnp.where(column == GRID - 1, 0.0, pltpu.roll(plain, count - 1, 0)).astype(bf16)

    def narrow_tile(i):
        span = pl.ds(pl.multiple_of(i * tile, tile), tile)
        mixed = jnp.concatenate(
            [att[d, :, span] for d in range(RING)], axis=0
        ).T
        block = tok[span, :].astype(f32) + jnp.dot(mixed, wproj[...], preferred_element_type=f32)
        thin = jnp.dot(block.astype(bf16), wn1[...], preferred_element_type=f32)
        thin = norm_rows(thin, g1_ref[...], 1e-06).astype(bf16).astype(f32)
        spread_columns(thin, pl.ds(pl.multiple_of(GRID + i * tile, GRID), tile))

    @pl.loop(0, 2)
    def _(i):
        narrow_tile(i * (tiles - 1))
    halo_copy(0).start()
    halo_copy(1).start()
    @pl.loop(1, tiles - 1)
    def _(i):
        narrow_tile(i)

    def conv_tile(i):
        total = None
        for row_off in range(3):
            at = pl.ds(pl.multiple_of(i * tile + row_off * GRID, GRID), tile)
            for col_off in range(3):
                tap = (row_off * 3 + col_off) * NECK
                part = jnp.dot(maps[col_off, at, :], wn2[tap : tap + NECK, :], preferred_element_type=f32)
                total = part if total is None else total + part
        emb_ref[pl.ds(pl.multiple_of(i * tile, tile), tile), :] = norm_rows(
            total, g2_ref[...], 1e-06
        )

    @pl.loop(1, tiles - 1)
    def _(i):
        conv_tile(i)

    halo_copy(0).wait_recv()
    halo_copy(1).wait_recv()
    above = halo[1].astype(f32) * (me > 0).astype(f32)
    below = halo[0].astype(f32) * (me < RING - 1).astype(f32)
    spread_columns(above, pl.ds(0, GRID))
    spread_columns(below, pl.ds(GRID + rows, GRID))

    @pl.loop(0, 2)
    def _(i):
        conv_tile(i * (tiles - 1))

    for kind in range(3):
        for head in range(2):
            for d in range(1, RING):
                qkv_copy(kind, head, d).wait_send()
    for head in range(2):
        for d in range(1, RING):
            out_copy(head, d).wait_send()
    halo_copy(0).wait_send()
    halo_copy(1).wait_send()
    width = ATTN_DIM // DEC_HEADS
    turn = 2.0 * math.pi
    px_row, py_row = pe_ref[0:1, :], pe_ref[1:2, :]
    grid_rows = rows // GRID
    col_angle = turn * (((iota((GRID, 128), 0).astype(f32) + 0.5) / GRID * 2.0 - 1.0) * px_row)
    row_no = iota((grid_rows, 128), 0) + me * grid_rows
    row_angle = turn * (((row_no.astype(f32) + 0.5) / GRID * 2.0 - 1.0) * py_row)
    col_sin, col_cos = jnp.sin(col_angle), jnp.cos(col_angle)
    row_sin, row_cos = jnp.sin(row_angle), jnp.cos(row_angle)
    key_w = dec_qkv_ref[1]
    value_w = dec_qkv_ref[2].astype(bf16)
    key_high, key_low = split(key_w)
    for r in range(grid_rows):
        span = pl.ds(r * GRID, GRID)
        rs, rc = row_sin[r : r + 1], row_cos[r : r + 1]
        code = jnp.concatenate(
            [col_sin * rc + col_cos * rs, col_cos * rc - col_sin * rs], axis=1
        )
        cell = emb_ref[span, :]
        high, low = split(cell + code)
        projected = dot(high, key_high) + (dot(high, key_low) + dot(low, key_high))
        k_high, k_low = split(projected)
        keys[span, 0:128] = k_high
        keys[span, 128:256] = k_low
        values[span, :] = dot(cell.astype(bf16), value_w).astype(bf16)

    @pl.loop(1, owners)
    def _(k):
        point_copy(k).wait_recv()

    row = iota((slots, owners * 8), 0)
    pick = (iota((slots, owners * 8), 1) == (row // CAP) * 8 + row % CAP).astype(bf16)
    picked = dot(pick, arrived[...].reshape(owners * 8, 128).astype(bf16))
    where_x = picked[:, 0:1] * 32.0 + picked[:, 1:2]
    where_y = picked[:, 2:3] * 32.0 + picked[:, 3:4]
    angle = turn * (
        ((where_x + 0.5) / IMG_SIDE * 2.0 - 1.0) * px_row + ((where_y + 0.5) / IMG_SIDE * 2.0 - 1.0) * py_row
    )
    query_tok = bias_ref[...] + jnp.concatenate([jnp.sin(angle), jnp.cos(angle)], axis=1)
    query = exact_dot(query_tok, dec_qkv_ref[0]) * (LOG2E / math.sqrt(width))
    head_of = iota((slots, 128), 1) // width
    mix = jnp.zeros((slots, 128), f32)
    lev = jnp.zeros((slots, 128), f32)
    for e in range(DEC_HEADS):
        q_high, q_low = split(jnp.where(head_of == e, query, 0.0))
        scores = lax.dot_general(
            jnp.concatenate([q_high, q_high], axis=1), keys[...], contract, preferred_element_type=f32
        ) + lax.dot_general(q_low, keys[:, 0:128], contract, preferred_element_type=f32)
        top = jnp.max(scores, axis=1, keepdims=True)
        weights = jnp.exp2(scores - top)
        total = jnp.sum(weights, axis=1, keepdims=True)
        part = dot(weights.astype(bf16), values[...]) / total
        mix = jnp.where(head_of == e, part, mix)
        lev = jnp.where(head_of == e, top + jnp.log(total) * LOG2E, lev)
    mixed[...] = mix.astype(bf16)
    level[...] = lev

    def stat_copy(kind, d):
        src, dst = ((mixed, got_mixed), (level, got_level))[kind]
        return pltpu.make_async_remote_copy(
            src_ref=src, dst_ref=dst.at[d],
            send_sem=stat_send.at[kind, d], recv_sem=stat_recv.at[kind, d],
            device_id={"tok": lax.rem(me + d, RING)}, device_id_type=MESH,
        )

    for d in (2, 1, 3):
        stat_copy(0, d).start()
        stat_copy(1, d).start()

    gain_col = jnp.sum(
        jnp.where(iota((UP1, UP1), 0) == iota((UP1, UP1), 1), up_gain_ref[...], 0.0), axis=1, keepdims=True
    )
    first_w = up1_ref[...].T.astype(bf16)
    second_w = up2_ref[...].T.astype(bf16)
    lanes = 256

    @pl.loop(0, rows // lanes)
    def _(i):
        span = pl.ds(pl.multiple_of(i * lanes, lanes), lanes)
        wide = lax.dot_general(
            first_w, emb_ref[span, :].astype(bf16), contract, preferred_element_type=f32
        )
        for g in range(4):
            part = wide[g * UP1 : (g + 1) * UP1]
            centred = part - jnp.mean(part, axis=0, keepdims=True)
            spread = jnp.mean(centred * centred, axis=0, keepdims=True)
            first = gelu(centred * lax.rsqrt(spread + 1e-06) * gain_col)
            ups[g, :, span] = gelu(dot(second_w, first.astype(bf16))).astype(bf16)

    for load in late:
        load.wait()
    for d in range(1, RING):
        stat_copy(0, d).wait_recv()
        stat_copy(1, d).wait_recv()
    levels = [lev] + [got_level[d] for d in range(1, RING)]
    parts = [mixed[...].astype(f32)] + [got_mixed[d].astype(f32) for d in range(1, RING)]
    peak = jnp.maximum(jnp.maximum(levels[0], levels[1]), jnp.maximum(levels[2], levels[3]))
    shares = [jnp.exp2(item - peak) for item in levels]
    cross = sum(s * p for s, p in zip(shares, parts)) / sum(shares)

    first_out = norm_rows(
        query_tok + dot(cross.astype(bf16), dec_out_ref[...].astype(bf16)), dec_gains_ref[0:1, :], 1e-05
    )
    hidden = jnp.maximum(dot(first_out.astype(bf16), mlp1[...].astype(bf16)), 0.0)
    second = norm_rows(
        first_out + dot(hidden.astype(bf16), mlp2[...].astype(bf16)), dec_gains_ref[1:2, :], 1e-05
    )
    vec = jnp.maximum(dot(second.astype(bf16), hyper[0].astype(bf16)), 0.0)
    vec = jnp.maximum(dot(vec.astype(bf16), hyper[1].astype(bf16)), 0.0)
    last = hyper_out_ref[...]
    vec = lax.dot_general(
        vec.astype(bf16), jnp.concatenate([last] * 4, axis=0).astype(bf16), contract, preferred_element_type=f32
    ).astype(bf16)
    big = owners * 16
    row = iota((big, slots), 0)
    repeat = (iota((big, slots), 1) == (row // 16) * CAP + row % CAP).astype(bf16)
    row = iota((big, 128), 0)
    stacked = jnp.where((row // CAP) % 4 == iota((big, 128), 1) // UP2, dot(repeat, vec), 0.0).astype(bf16)

    def mask_copy(g, k):
        to = partner(img, k)
        return pltpu.make_async_remote_copy(
            src_ref=ready.at[g, to], dst_ref=received.at[g, img],
            send_sem=mask_send.at[g, k], recv_sem=mask_recv.at[g, k],
            device_id={"img": to}, device_id_type=MESH,
        )

    for g in range(4):
        ready[g] = dot(stacked, ups[g]).astype(bf16).reshape(owners, 16, rows)

        @pl.loop(1, owners)
        def _(k):
            mask_copy(g, lax.rem(k * 13, owners)).start()
        received[g, img] = ready[g, img]

    half = slots // 2
    diagonal = iota((half, half), 0) == iota((half, half), 1)
    spot = jnp.sum(
        jnp.where(diagonal, (place[0] * 16 + place[1]).astype(f32), 0.0), axis=1, keepdims=True
    ).astype(jnp.int32)
    for k in range(4):
        chooser[k * half : (k + 1) * half, :] = (iota((half, owners * 16), 1) == spot + k * CAP).astype(bf16)
    row, col = iota((512, 512), 0), iota((512, 512), 1)
    inside = row % 128
    mover_ref[...] = (col == (inside // GRID) * 256 + (inside % GRID) * 4 + row // 128).astype(bf16)

    @pl.loop(1, owners)
    def _(k):
        point_copy(k).wait_send()
    for d in range(1, RING):
        stat_copy(0, d).wait_send()
        stat_copy(1, d).wait_send()
    for g in range(4):
        @pl.loop(1, owners)
        def _(k):
            mask_copy(g, k).wait_recv()
        chosen_ref[g] = dot(chooser[...], received[g].reshape(owners * 16, rows)).astype(bf16)
    for g in range(4):
        @pl.loop(1, owners)
        def _(k):
            mask_copy(g, k).wait_send()


def trunk(
    picture, ln_gain, w_qkv, w_proj, w_neck1, gain1, w_neck2, gain2, pe_matrix, query_bias, dec_qkv,
    dec_out, dec_gains, w_mlp1, w_mlp2, w_hyper, w_hyper_out, w_up1, up_gain, w_up2, req_image, points, owners,
):
    rows, width = picture.shape
    anywhere = pl.BlockSpec(memory_space=pl.ANY)
    local = pl.BlockSpec(memory_space=pltpu.VMEM)
    inner = HEADS * HDIM
    slots = owners * CAP
    dma = pltpu.SemaphoreType.DMA
    return pl.pallas_call(
        trunk_kernel,
        out_shape=(
            jax.ShapeDtypeStruct((4, slots * 2, rows), bf16),
            jax.ShapeDtypeStruct((512, 512), bf16),
        ),
        in_specs=[anywhere, local, anywhere, anywhere, anywhere, local, anywhere, local]
        + [local] * 7 + [anywhere] * 3 + [local] * 4,
        out_specs=(local, local),
        scratch_shapes=[
            pltpu.VMEM((rows, width), bf16),
            pltpu.VMEM(w_qkv.shape, bf16),
            pltpu.VMEM(w_proj.shape, bf16),
            pltpu.VMEM(w_neck1.shape, bf16),
            pltpu.VMEM(w_neck2.shape, bf16),
            pltpu.VMEM((rows, width), bf16),
            pltpu.VMEM((3 * inner, rows), bf16),
            pltpu.VMEM((3, 2, RING, HDIM, rows), bf16),
            pltpu.VMEM((RING, rows, 128), bf16),
            pltpu.VMEM((2, RING, HDIM, rows), bf16),
            pltpu.VMEM((RING, 2 * HDIM, rows), bf16),
            pltpu.VMEM((3, rows + 2 * GRID, NECK), bf16),
            pltpu.VMEM((2, GRID, NECK), bf16),
            dma((11,)),
            dma((3, 2, RING)),
            dma((3, 2, RING)),
            dma((2, RING)),
            dma((2, RING)),
            dma((2,)),
            dma((2,)),
            pltpu.VMEM((rows, NECK), f32),
            pltpu.VMEM((owners, 8, 128), f32),
            pltpu.VMEM((owners, 8, 128), f32),
            pltpu.VMEM(w_mlp1.shape, f32),
            pltpu.VMEM(w_mlp2.shape, f32),
            pltpu.VMEM(w_hyper.shape, f32),
            pltpu.VMEM((rows, 256), bf16),
            pltpu.VMEM((rows, 128), bf16),
            pltpu.VMEM((slots, 128), bf16),
            pltpu.VMEM((slots, 128), f32),
            pltpu.VMEM((RING, slots, 128), bf16),
            pltpu.VMEM((RING, slots, 128), f32),
            pltpu.VMEM((4, 128, rows), bf16),
            pltpu.VMEM((4, owners, 16, rows), bf16),
            pltpu.VMEM((4, owners, 16, rows), bf16),
            pltpu.VMEM((slots * 2, owners * 16), bf16),
            dma((3,)),
            dma((owners,)),
            dma((owners,)),
            dma((2, RING)),
            dma((2, RING)),
            dma((4, owners)),
            dma((4, owners)),
        ],
        compiler_params=pltpu.CompilerParams(
            collective_id=0, has_side_effects=True, vmem_limit_bytes=62 * 1024 * 1024
        ),
    )(
        picture, ln_gain.reshape(1, -1), w_qkv, w_proj, w_neck1, gain1.reshape(1, -1), w_neck2,
        gain2.reshape(1, -1), req_image.T, points.T, pe_matrix, query_bias.reshape(1, -1), dec_qkv,
        dec_out, dec_gains, w_mlp1, w_mlp2, w_hyper, w_hyper_out.T, w_up1, up_gain.reshape(1, -1), w_up2,
    )


def interleave_kernel(chosen_ref, mover_ref, out_ref):
    slots = out_ref.shape[0]
    sub = chosen_ref.shape[2] // 128
    for p in range(sub):
        span = slice(p * 128, (p + 1) * 128)
        sides = [
            jnp.concatenate(
                [
                    chosen_ref[dr * 2 + dc, (er * 2 + ec) * slots : (er * 2 + ec + 1) * slots, span]
                    for dc in range(2)
                    for ec in range(2)
                ],
                axis=1,
            )
            for dr in range(2)
            for er in range(2)
        ]
        lines = dot(jnp.concatenate(sides, axis=0), mover_ref[...])
        for j in range(4):
            for r in range(2):
                line = (p * 8 + r * 4 + j) * 256
                out_ref[:, line : line + 256] = lines[j * slots : (j + 1) * slots, r * 256 : (r + 1) * 256]


def interleave(chosen, mover):
    groups, tall, rows = chosen.shape
    slots = tall // 4
    lanes = 256
    return pl.pallas_call(
        interleave_kernel,
        out_shape=jax.ShapeDtypeStruct((slots, rows * 16), f32),
        grid=(rows // lanes,),
        in_specs=[
            pl.BlockSpec((groups, tall, lanes), lambda i: (0, 0, i)),
            pl.BlockSpec((512, 512), lambda i: (0, 0)),
        ],
        out_specs=pl.BlockSpec((slots, lanes * 16), lambda i: (0, i)),
        compiler_params=pltpu.CompilerParams(vmem_limit_bytes=56 * 1024 * 1024),
    )(chosen, mover)


def body(tokens, *others):
    return interleave(*trunk(tokens[0], *others, lax.axis_size("img")))


def solution(mesh):
    placed = (
        P("img", "tok", None),
        P(),
        P(),
        P(),
        P(),
        P(),
        P(),
        P(),
        P(),
        P(),
        P(),
        P(),
        P(),
        P(),
        P(),
        P(),
        P(),
        P(),
        P(),
        P(),
        P("img", None),
        P("img", None),
    )
    return jax.shard_map(
        body, mesh=mesh, in_specs=placed, out_specs=P("img", "tok"), check_vma=False
    )
```

```python
import math

import jax
import jax.numpy as jnp
from jax import lax
from jax.experimental import pallas as pl
from jax.experimental.pallas import tpu as pltpu
from jax.sharding import PartitionSpec as P

HEADS = 8
HDIM = 80
GRID = 64
NECK = 256
ATTN_DIM = 128
DEC_HEADS = 8
UP1 = 64
UP2 = 32
IMG_SIDE = 1024
CAP = 4
RING = 4
MESH = pl.DeviceIdType.MESH
bf16 = jnp.bfloat16
f32 = jnp.float32
LOG2E = math.log2(math.e)
highest_precision = lax.Precision.HIGHEST


def norm_rows(x, gain, eps):
    centred = x - jnp.mean(x, axis=-1, keepdims=True)
    spread = jnp.mean(centred * centred, axis=-1, keepdims=True)
    return centred * lax.rsqrt(spread + eps) * gain


def iota(shape, axis):
    return lax.broadcasted_iota(jnp.int32, shape, axis)


def dot(a, b):
    return jnp.dot(a, b, preferred_element_type=f32)


def exact_dot(a, b):
    return jnp.dot(a, b, preferred_element_type=f32, precision=highest_precision)


def gelu(x):
    return 0.5 * x * (1.0 + lax.erf(x * math.sqrt(0.5)))


def request_places(targets, owners):
    count = targets.shape[1]
    match = (iota((owners, count), 0) == targets).astype(f32)
    earlier = (iota((count, count), 0) < iota((count, count), 1)).astype(bf16)
    seen = dot(match.astype(bf16), earlier)
    return targets, jnp.sum(seen * match, axis=0, keepdims=True).astype(jnp.int32)


def partner(img, k):
    dx, dy, dc = k // 8, (k // 2) % 4, k % 2
    x, y, core = img // 8, (img // 2) % 4, img % 2
    return lax.rem(x + dx, 4) * 8 + lax.rem(y + dy, 4) * 2 + lax.rem(core + dc, 2)


def split(x):
    high = x.astype(bf16)
    return high, (x - high.astype(f32)).astype(bf16)


def trunk_kernel(
    tok_hbm, gain_ref, wqkv_hbm, wproj_hbm, wn1_hbm, g1_ref, wn2_hbm, g2_ref,
    req_ref, points_ref, pe_ref, bias_ref, dec_qkv_ref, dec_out_ref, dec_gains_ref,
    mlp1_hbm, mlp2_hbm, hyper_hbm, hyper_out_ref, up1_ref, up_gain_ref, up2_ref,
    chosen_hbm, mover_hbm,
    tok, wqkv, wproj, wn1, wn2, normed, loc, got, vrows, outs, att, maps, halo,
    load_sem, qkv_send, qkv_recv, out_send, out_recv, halo_send, halo_recv,
    emb_ref, outgoing, arrived, mlp1, mlp2, hyper, keys, values, mixed, level, got_mixed, got_level, ups,
    ready, received, chooser, chosen, mover,
    late_sem, point_send, point_recv, stat_send, stat_recv, mask_send, mask_recv, leave_sem,
):
    me = lax.axis_index("tok")
    rows = tok.shape[0]
    two = 2 * HDIM
    slots = received.shape[1] * CAP
    contract = (((1,), (1,)), ((), ()))
    inner = HEADS * HDIM
    tile = 256
    tiles = rows // tile
    qblock = 512

    loads = [
        pltpu.make_async_copy(tok_hbm.at[pl.ds(i * tile, tile)], tok.at[pl.ds(i * tile, tile)], load_sem.at[i])
        for i in range(tiles)
    ]
    columns = [pl.ds(kind * inner, inner) for kind in range(3)]
    weights_in = [
        pltpu.make_async_copy(wqkv_hbm.at[:, columns[kind]], wqkv.at[:, columns[kind]], load_sem.at[11 + kind])
        for kind in range(3)
    ]
    loads.append(weights_in[1])
    loads.append(pltpu.make_async_copy(wn1_hbm, wn1, load_sem.at[5]))
    loads.append(pltpu.make_async_copy(wn2_hbm, wn2, load_sem.at[6]))
    loads.append(weights_in[2])
    loads.append(weights_in[0])
    for d in range(RING):
        owner = lax.rem(me + d, RING)
        loads.append(
            pltpu.make_async_copy(
                wproj_hbm.at[pl.ds(pl.multiple_of(owner * two, 32), two)],
                wproj.at[pl.ds(d * two, two)],
                load_sem.at[7 + d],
            )
        )
    late = [
        pltpu.make_async_copy(a, b, late_sem.at[i])
        for i, (a, b) in enumerate(((mlp1_hbm, mlp1), (mlp2_hbm, mlp2), (hyper_hbm, hyper)))
    ]
    for load in loads + late:
        load.start()

    img = lax.axis_index("img")
    owners = received.shape[1]
    barrier = pltpu.get_barrier_semaphore()
    for d in range(1, RING):
        pl.semaphore_signal(
            barrier, inc=1, device_id={"tok": lax.rem(me + d, RING)}, device_id_type=MESH
        )

    @pl.loop(1, owners)
    def _(k):
        pl.semaphore_signal(barrier, inc=1, device_id={"img": partner(img, k)}, device_id_type=MESH)

    scale = math.log2(math.e) / math.sqrt(HDIM)

    def qkv_copy(kind, head, d):
        owner = lax.rem(me + d, RING)
        first = pl.multiple_of(kind * inner + owner * two + head * HDIM, 16)
        return pltpu.make_async_remote_copy(
            src_ref=loc.at[pl.ds(first, HDIM)],
            dst_ref=got.at[kind, head, d],
            send_sem=qkv_send.at[kind, head, d],
            recv_sem=qkv_recv.at[kind, head, d],
            device_id={"tok": owner},
            device_id_type=MESH,
        )

    def project(kind, first, last):
        @pl.loop(first, last)
        def _(i):
            span = pl.ds(pl.multiple_of(i * tile, tile), tile)
            part = jnp.dot(
                normed[span, :], wqkv[:, kind * inner : (kind + 1) * inner], preferred_element_type=f32
            )
            if kind == 0:
                part = part * scale
            loc[kind * inner : (kind + 1) * inner, span] = part.astype(bf16).T

    def early_keys(d, part):
        owner = lax.rem(me + d, RING)
        first = pl.multiple_of(inner + owner * two, 16)
        span = pl.ds(part * (rows // 2), rows // 2)
        return pltpu.make_async_remote_copy(
            src_ref=loc.at[pl.ds(first, HDIM), span],
            dst_ref=got.at[1, 0, d, :, span],
            send_sem=qkv_send.at[1, 0, d],
            recv_sem=qkv_recv.at[1, 0, d],
            device_id={"tok": owner},
            device_id_type=MESH,
        )

    for part in range(2):
        for i in range(part * tiles // 2, (part + 1) * tiles // 2):
            loads[i].wait()
            span = pl.ds(i * tile, tile)
            normed[span, :] = norm_rows(tok[span, :].astype(f32), gain_ref[...].reshape(1, -1), 1e-06).astype(bf16)
        if part == 0:
            weights_in[1].wait()
        project(1, part * tiles // 2, (part + 1) * tiles // 2)
        if part == 0:
            pl.semaphore_wait(barrier, owners - 1 + RING - 1)
        for d in (1, 3, 2):
            early_keys(d, part).start()
    for kind in (2, 0):
        weights_in[kind].wait()
        project(kind, 0, tiles)
        for d in (1, 3, 2):
            qkv_copy(kind, 0, d).start()
    for kind in (1, 2, 0):
        for d in (1, 3, 2):
            qkv_copy(kind, 1, d).start()
    place = request_places(req_ref[...], owners)
    placing = (iota((owners * 8, slots // 2), 0) == place[0] * 8 + place[1]).astype(bf16)
    line = iota((128, slots // 2), 0)
    across, down = points_ref[0:1, :], points_ref[1:2, :]
    parts = jnp.where(
        line == 0,
        across // 32,
        jnp.where(line == 1, across % 32, jnp.where(line == 2, down // 32, jnp.where(line == 3, down % 32, 0))),
    )
    outgoing[...] = lax.dot_general(
        placing, parts.astype(f32).astype(bf16), contract, preferred_element_type=f32
    ).reshape(owners, 8, 128)

    def point_copy(k):
        to = partner(img, k)
        return pltpu.make_async_remote_copy(
            src_ref=outgoing.at[to], dst_ref=arrived.at[img],
            send_sem=point_send.at[k], recv_sem=point_recv.at[k],
            device_id={"img": to}, device_id_type=MESH,
        )

    for kind in range(3):
        for head in range(2):
            first = pl.multiple_of(kind * inner + me * two + head * HDIM, 16)
            got[kind, head, 0] = loc[pl.ds(first, HDIM), :]

    @pl.loop(1, owners)
    def _(k):
        point_copy(k).start()
    arrived[img] = outgoing[img]

    def out_copy(head, d):
        target = lax.rem(me - d + RING, RING)
        return pltpu.make_async_remote_copy(
            src_ref=outs.at[head, d],
            dst_ref=att.at[d, pl.ds(pl.multiple_of(head * HDIM, 16), HDIM)],
            send_sem=out_send.at[head, d],
            recv_sem=out_recv.at[head, d],
            device_id={"tok": target},
            device_id_type=MESH,
        )

    filler = (lax.broadcasted_iota(jnp.int32, (48, rows), 0) == 0).astype(bf16)
    halves = rows // qblock

    @pl.loop(0, 2)
    def _(head):
        for d in range(1, RING):
            qkv_copy(1, head, d).wait_recv()
            qkv_copy(2, head, d).wait_recv()
        for d in range(RING):
            vrows[d] = jnp.concatenate([got[2, head, d], filler], axis=0).T

        @pl.loop(0, RING)
        def _(turn):
            slot = lax.rem(turn + head, RING)

            @pl.when(slot > 0)
            def _():
                qkv_copy(0, head, slot).wait_recv()

            @pl.loop(0, halves)
            def _(half):
                span = pl.ds(pl.multiple_of(half * qblock, qblock), qblock)
                query = got[0, head, slot, :, span].T

                def scores(d):
                    return jnp.dot(query, got[1, head, d], preferred_element_type=f32)

                now = scores(0)
                top = None
                for d in range(RING):
                    ahead = scores(d + 1) if d + 1 < RING else None
                    here = jnp.max(now, axis=1, keepdims=True)
                    fresh = here if top is None else jnp.maximum(top, here)
                    weights = jnp.exp2(now - fresh).astype(bf16)
                    part = jnp.dot(weights, vrows[d], preferred_element_type=f32)
                    total = part if top is None else total * jnp.exp2(top - fresh) + part
                    top, now = fresh, ahead
                final = (total * (1.0 / total[:, HDIM : HDIM + 1])).astype(bf16).T[:HDIM]
                outs[head, slot, :, span] = final

            @pl.when(slot > 0)
            def _():
                out_copy(head, slot).start()

            @pl.when(slot == 0)
            def _():
                att[0, pl.ds(pl.multiple_of(head * HDIM, 16), HDIM), :] = outs[head, 0]

    for d in range(1, RING):
        for head in range(2):
            out_copy(head, d).wait_recv()
    for load in loads[5:7] + loads[9:]:
        load.wait()

    def halo_copy(side):
        start = GRID + (0 if side == 0 else rows - GRID)
        return pltpu.make_async_remote_copy(
            src_ref=maps.at[1, pl.ds(start, GRID)],
            dst_ref=halo.at[side],
            send_sem=halo_send.at[side],
            recv_sem=halo_recv.at[side],
            device_id={"tok": lax.rem(me + (RING - 1 if side == 0 else 1), RING)},
            device_id_type=MESH,
        )

    def spread_columns(plain, at):
        count = plain.shape[0]
        column = lax.broadcasted_iota(jnp.int32, (count, NECK), 0) % GRID
        maps[1, at, :] = plain.astype(bf16)
        maps[0, at, :] = jnp.where(column == 0, 0.0, pltpu.roll(plain, 1, 0)).astype(bf16)
        maps[2, at, :] = jnp.where(column == GRID - 1, 0.0, pltpu.roll(plain, count - 1, 0)).astype(bf16)

    def narrow_tile(i):
        span = pl.ds(pl.multiple_of(i * tile, tile), tile)
        mixed = jnp.concatenate(
            [att[d, :, span] for d in range(RING)], axis=0
        ).T
        block = tok[span, :].astype(f32) + jnp.dot(mixed, wproj[...], preferred_element_type=f32)
        thin = jnp.dot(block.astype(bf16), wn1[...], preferred_element_type=f32)
        thin = norm_rows(thin, g1_ref[...], 1e-06).astype(bf16).astype(f32)
        spread_columns(thin, pl.ds(pl.multiple_of(GRID + i * tile, GRID), tile))

    @pl.loop(0, 2)
    def _(i):
        narrow_tile(i * (tiles - 1))
    halo_copy(0).start()
    halo_copy(1).start()
    @pl.loop(1, tiles - 1)
    def _(i):
        narrow_tile(i)

    def conv_tile(i):
        total = None
        for row_off in range(3):
            at = pl.ds(pl.multiple_of(i * tile + row_off * GRID, GRID), tile)
            for col_off in range(3):
                tap = (row_off * 3 + col_off) * NECK
                part = jnp.dot(maps[col_off, at, :], wn2[tap : tap + NECK, :], preferred_element_type=f32)
                total = part if total is None else total + part
        emb_ref[pl.ds(pl.multiple_of(i * tile, tile), tile), :] = norm_rows(
            total, g2_ref[...], 1e-06
        )

    @pl.loop(1, tiles - 1)
    def _(i):
        conv_tile(i)

    halo_copy(0).wait_recv()
    halo_copy(1).wait_recv()
    above = halo[1].astype(f32) * (me > 0).astype(f32)
    below = halo[0].astype(f32) * (me < RING - 1).astype(f32)
    spread_columns(above, pl.ds(0, GRID))
    spread_columns(below, pl.ds(GRID + rows, GRID))

    @pl.loop(0, 2)
    def _(i):
        conv_tile(i * (tiles - 1))

    for kind in range(3):
        for head in range(2):
            for d in range(1, RING):
                qkv_copy(kind, head, d).wait_send()
    for head in range(2):
        for d in range(1, RING):
            out_copy(head, d).wait_send()
    halo_copy(0).wait_send()
    halo_copy(1).wait_send()
    width = ATTN_DIM // DEC_HEADS
    turn = 2.0 * math.pi
    px_row, py_row = pe_ref[0:1, :], pe_ref[1:2, :]
    grid_rows = rows // GRID
    col_angle = turn * (((iota((GRID, 128), 0).astype(f32) + 0.5) / GRID * 2.0 - 1.0) * px_row)
    row_no = iota((grid_rows, 128), 0) + me * grid_rows
    row_angle = turn * (((row_no.astype(f32) + 0.5) / GRID * 2.0 - 1.0) * py_row)
    col_sin, col_cos = jnp.sin(col_angle), jnp.cos(col_angle)
    row_sin, row_cos = jnp.sin(row_angle), jnp.cos(row_angle)
    key_w = dec_qkv_ref[1]
    value_w = dec_qkv_ref[2].astype(bf16)
    key_high, key_low = split(key_w)
    for r in range(grid_rows):
        span = pl.ds(r * GRID, GRID)
        rs, rc = row_sin[r : r + 1], row_cos[r : r + 1]
        code = jnp.concatenate(
            [col_sin * rc + col_cos * rs, col_cos * rc - col_sin * rs], axis=1
        )
        cell = emb_ref[span, :]
        high, low = split(cell + code)
        projected = dot(high, key_high) + (dot(high, key_low) + dot(low, key_high))
        k_high, k_low = split(projected)
        keys[span, 0:128] = k_high
        keys[span, 128:256] = k_low
        values[span, :] = dot(cell.astype(bf16), value_w).astype(bf16)

    @pl.loop(1, owners)
    def _(k):
        point_copy(k).wait_recv()

    row = iota((slots, owners * 8), 0)
    pick = (iota((slots, owners * 8), 1) == (row // CAP) * 8 + row % CAP).astype(bf16)
    picked = dot(pick, arrived[...].reshape(owners * 8, 128).astype(bf16))
    where_x = picked[:, 0:1] * 32.0 + picked[:, 1:2]
    where_y = picked[:, 2:3] * 32.0 + picked[:, 3:4]
    angle = turn * (
        ((where_x + 0.5) / IMG_SIDE * 2.0 - 1.0) * px_row + ((where_y + 0.5) / IMG_SIDE * 2.0 - 1.0) * py_row
    )
    query_tok = bias_ref[...] + jnp.concatenate([jnp.sin(angle), jnp.cos(angle)], axis=1)
    query = exact_dot(query_tok, dec_qkv_ref[0]) * (LOG2E / math.sqrt(width))
    head_of = iota((slots, 128), 1) // width
    mix = jnp.zeros((slots, 128), f32)
    lev = jnp.zeros((slots, 128), f32)
    group = 4
    for first in range(0, DEC_HEADS, group):
        heads = range(first, first + group)
        q_high, q_low = split(jnp.concatenate([jnp.where(head_of == e, query, 0.0) for e in heads], axis=0))
        scores = lax.dot_general(
            jnp.concatenate([q_high, q_high], axis=1), keys[...], contract, preferred_element_type=f32
        ) + lax.dot_general(q_low, keys[:, 0:128], contract, preferred_element_type=f32)
        top = jnp.max(scores, axis=1, keepdims=True)
        weights = jnp.exp2(scores - top)
        total = jnp.sum(weights, axis=1, keepdims=True)
        part = dot(weights.astype(bf16), values[...]) / total
        height = top + jnp.log(total) * LOG2E
        for j, e in enumerate(heads):
            at = slice(j * slots, (j + 1) * slots)
            mix = jnp.where(head_of == e, part[at], mix)
            lev = jnp.where(head_of == e, height[at], lev)
    mixed[...] = mix.astype(bf16)
    level[...] = lev

    def stat_copy(kind, d):
        src, dst = ((mixed, got_mixed), (level, got_level))[kind]
        return pltpu.make_async_remote_copy(
            src_ref=src, dst_ref=dst.at[d],
            send_sem=stat_send.at[kind, d], recv_sem=stat_recv.at[kind, d],
            device_id={"tok": lax.rem(me + d, RING)}, device_id_type=MESH,
        )

    for d in (2, 1, 3):
        stat_copy(0, d).start()
        stat_copy(1, d).start()

    gain_col = jnp.sum(
        jnp.where(iota((UP1, UP1), 0) == iota((UP1, UP1), 1), up_gain_ref[...], 0.0), axis=1, keepdims=True
    )
    first_w = up1_ref[...].T.astype(bf16)
    second_w = up2_ref[...].T.astype(bf16)
    lanes = 256

    @pl.loop(0, rows // lanes)
    def _(i):
        span = pl.ds(pl.multiple_of(i * lanes, lanes), lanes)
        wide = lax.dot_general(
            first_w, emb_ref[span, :].astype(bf16), contract, preferred_element_type=f32
        )
        for g in range(4):
            part = wide[g * UP1 : (g + 1) * UP1]
            centred = part - jnp.mean(part, axis=0, keepdims=True)
            spread = jnp.mean(centred * centred, axis=0, keepdims=True)
            first = gelu(centred * lax.rsqrt(spread + 1e-06) * gain_col)
            ups[g, :, span] = gelu(dot(second_w, first.astype(bf16))).astype(bf16)

    for load in late:
        load.wait()
    for d in range(1, RING):
        stat_copy(0, d).wait_recv()
        stat_copy(1, d).wait_recv()
    levels = [lev] + [got_level[d] for d in range(1, RING)]
    parts = [mixed[...].astype(f32)] + [got_mixed[d].astype(f32) for d in range(1, RING)]
    peak = jnp.maximum(jnp.maximum(levels[0], levels[1]), jnp.maximum(levels[2], levels[3]))
    shares = [jnp.exp2(item - peak) for item in levels]
    cross = sum(s * p for s, p in zip(shares, parts)) / sum(shares)

    first_out = norm_rows(
        query_tok + dot(cross.astype(bf16), dec_out_ref[...].astype(bf16)), dec_gains_ref[0:1, :], 1e-05
    )
    hidden = jnp.maximum(dot(first_out.astype(bf16), mlp1[...].astype(bf16)), 0.0)
    second = norm_rows(
        first_out + dot(hidden.astype(bf16), mlp2[...].astype(bf16)), dec_gains_ref[1:2, :], 1e-05
    )
    vec = jnp.maximum(dot(second.astype(bf16), hyper[0].astype(bf16)), 0.0)
    vec = jnp.maximum(dot(vec.astype(bf16), hyper[1].astype(bf16)), 0.0)
    last = hyper_out_ref[...]
    vec = lax.dot_general(
        vec.astype(bf16), jnp.concatenate([last] * 4, axis=0).astype(bf16), contract, preferred_element_type=f32
    ).astype(bf16)
    big = owners * 16
    row = iota((big, slots), 0)
    repeat = (iota((big, slots), 1) == (row // 16) * CAP + row % CAP).astype(bf16)
    row = iota((big, 128), 0)
    stacked = jnp.where((row // CAP) % 4 == iota((big, 128), 1) // UP2, dot(repeat, vec), 0.0).astype(bf16)

    def mask_copy(g, k):
        to = partner(img, k)
        return pltpu.make_async_remote_copy(
            src_ref=ready.at[g, to], dst_ref=received.at[g, img],
            send_sem=mask_send.at[g, k], recv_sem=mask_recv.at[g, k],
            device_id={"img": to}, device_id_type=MESH,
        )

    for g in range(4):
        ready[g] = dot(stacked, ups[g]).astype(bf16).reshape(owners, 16, rows)

        @pl.loop(1, owners)
        def _(k):
            mask_copy(g, lax.rem(k * 13, owners)).start()
        received[g, img] = ready[g, img]

    half = slots // 2
    diagonal = iota((half, half), 0) == iota((half, half), 1)
    spot = jnp.sum(
        jnp.where(diagonal, (place[0] * 16 + place[1]).astype(f32), 0.0), axis=1, keepdims=True
    ).astype(jnp.int32)
    for k in range(4):
        chooser[k * half : (k + 1) * half, :] = (iota((half, owners * 16), 1) == spot + k * CAP).astype(bf16)
    row, col = iota((512, 512), 0), iota((512, 512), 1)
    inside = row % 128
    mover[...] = (col == (inside // GRID) * 256 + (inside % GRID) * 4 + row // 128).astype(bf16)

    @pl.loop(1, owners)
    def _(k):
        point_copy(k).wait_send()
    for d in range(1, RING):
        stat_copy(0, d).wait_send()
        stat_copy(1, d).wait_send()
    leaving = [pltpu.make_async_copy(mover, mover_hbm, leave_sem.at[4])]
    leaving[0].start()
    for g in range(4):
        @pl.loop(1, owners)
        def _(k):
            mask_copy(g, k).wait_recv()
        chosen[g] = dot(chooser[...], received[g].reshape(owners * 16, rows)).astype(bf16)
        leaving.append(pltpu.make_async_copy(chosen.at[g], chosen_hbm.at[g], leave_sem.at[g]))
        leaving[-1].start()
    for g in range(4):
        @pl.loop(1, owners)
        def _(k):
            mask_copy(g, k).wait_send()
    for copy in leaving:
        copy.wait()


def trunk(
    picture, ln_gain, w_qkv, w_proj, w_neck1, gain1, w_neck2, gain2, pe_matrix, query_bias, dec_qkv,
    dec_out, dec_gains, w_mlp1, w_mlp2, w_hyper, w_hyper_out, w_up1, up_gain, w_up2, req_image, points, owners,
):
    rows, width = picture.shape
    anywhere = pl.BlockSpec(memory_space=pl.ANY)
    local = pl.BlockSpec(memory_space=pltpu.VMEM)
    inner = HEADS * HDIM
    slots = owners * CAP
    dma = pltpu.SemaphoreType.DMA
    return pl.pallas_call(
        trunk_kernel,
        out_shape=(
            jax.ShapeDtypeStruct((4, slots * 2, rows), bf16),
            jax.ShapeDtypeStruct((512, 512), bf16),
        ),
        in_specs=[anywhere, local, anywhere, anywhere, anywhere, local, anywhere, local]
        + [local] * 7 + [anywhere] * 3 + [local] * 4,
        out_specs=(anywhere, anywhere),
        scratch_shapes=[
            pltpu.VMEM((rows, width), bf16),
            pltpu.VMEM(w_qkv.shape, bf16),
            pltpu.VMEM(w_proj.shape, bf16),
            pltpu.VMEM(w_neck1.shape, bf16),
            pltpu.VMEM(w_neck2.shape, bf16),
            pltpu.VMEM((rows, width), bf16),
            pltpu.VMEM((3 * inner, rows), bf16),
            pltpu.VMEM((3, 2, RING, HDIM, rows), bf16),
            pltpu.VMEM((RING, rows, 128), bf16),
            pltpu.VMEM((2, RING, HDIM, rows), bf16),
            pltpu.VMEM((RING, 2 * HDIM, rows), bf16),
            pltpu.VMEM((3, rows + 2 * GRID, NECK), bf16),
            pltpu.VMEM((2, GRID, NECK), bf16),
            dma((14,)),
            dma((3, 2, RING)),
            dma((3, 2, RING)),
            dma((2, RING)),
            dma((2, RING)),
            dma((2,)),
            dma((2,)),
            pltpu.VMEM((rows, NECK), f32),
            pltpu.VMEM((owners, 8, 128), f32),
            pltpu.VMEM((owners, 8, 128), f32),
            pltpu.VMEM(w_mlp1.shape, f32),
            pltpu.VMEM(w_mlp2.shape, f32),
            pltpu.VMEM(w_hyper.shape, f32),
            pltpu.VMEM((rows, 256), bf16),
            pltpu.VMEM((rows, 128), bf16),
            pltpu.VMEM((slots, 128), bf16),
            pltpu.VMEM((slots, 128), f32),
            pltpu.VMEM((RING, slots, 128), bf16),
            pltpu.VMEM((RING, slots, 128), f32),
            pltpu.VMEM((4, 128, rows), bf16),
            pltpu.VMEM((4, owners, 16, rows), bf16),
            pltpu.VMEM((4, owners, 16, rows), bf16),
            pltpu.VMEM((slots * 2, owners * 16), bf16),
            pltpu.VMEM((4, slots * 2, rows), bf16),
            pltpu.VMEM((512, 512), bf16),
            dma((3,)),
            dma((owners,)),
            dma((owners,)),
            dma((2, RING)),
            dma((2, RING)),
            dma((4, owners)),
            dma((4, owners)),
            dma((5,)),
        ],
        compiler_params=pltpu.CompilerParams(
            collective_id=0, has_side_effects=True, vmem_limit_bytes=62 * 1024 * 1024
        ),
    )(
        picture, ln_gain, w_qkv, w_proj, w_neck1, gain1.reshape(1, -1), w_neck2,
        gain2.reshape(1, -1), req_image.T, points.T, pe_matrix, query_bias.reshape(1, -1), dec_qkv,
        dec_out, dec_gains, w_mlp1, w_mlp2, w_hyper, w_hyper_out.T, w_up1, up_gain.reshape(1, -1), w_up2,
    )


def interleave_kernel(chosen_ref, mover_ref, out_ref):
    slots = out_ref.shape[0]
    sub = chosen_ref.shape[2] // 128
    sides = [
        jnp.concatenate(
            [
                chosen_ref[
                    dr * 2 + dc, (er * 2 + ec) * slots : (er * 2 + ec + 1) * slots, p * 128 : (p + 1) * 128
                ]
                for dc in range(2)
                for ec in range(2)
            ],
            axis=1,
        )
        for p in range(sub)
        for dr in range(2)
        for er in range(2)
    ]
    lines = dot(jnp.concatenate(sides, axis=0), mover_ref[...])
    for p in range(sub):
        for j in range(4):
            at = slice((p * 4 + j) * slots, (p * 4 + j + 1) * slots)
            for r in range(2):
                line = (p * 8 + r * 4 + j) * 256
                out_ref[:, line : line + 256] = lines[at, r * 256 : (r + 1) * 256]


def interleave(chosen, mover):
    groups, tall, rows = chosen.shape
    slots = tall // 4
    lanes = 256
    return pl.pallas_call(
        interleave_kernel,
        out_shape=jax.ShapeDtypeStruct((slots, rows * 16), f32),
        grid=(rows // lanes,),
        in_specs=[
            pl.BlockSpec((groups, tall, lanes), lambda i: (0, 0, i)),
            pl.BlockSpec((512, 512), lambda i: (0, 0)),
        ],
        out_specs=pl.BlockSpec((slots, lanes * 16), lambda i: (0, i)),
        compiler_params=pltpu.CompilerParams(vmem_limit_bytes=56 * 1024 * 1024),
    )(chosen, mover)


def body(tokens, *others):
    return interleave(*trunk(tokens[0], *others, lax.axis_size("img")))


def solution(mesh):
    placed = (
        P("img", "tok", None),
        P(),
        P(),
        P(),
        P(),
        P(),
        P(),
        P(),
        P(),
        P(),
        P(),
        P(),
        P(),
        P(),
        P(),
        P(),
        P(),
        P(),
        P(),
        P(),
        P("img", None),
        P("img", None),
    )
    return jax.shard_map(
        body, mesh=mesh, in_specs=placed, out_specs=P("img", "tok"), check_vma=False
    )
```

```python
import math

import jax
import jax.numpy as jnp
from jax import lax
from jax.experimental import pallas as pl
from jax.experimental.pallas import tpu as pltpu
from jax.sharding import PartitionSpec as P

HEADS = 8
HDIM = 80
GRID = 64
NECK = 256
ATTN_DIM = 128
DEC_HEADS = 8
UP1 = 64
UP2 = 32
IMG_SIDE = 1024
CAP = 4
RING = 4
MESH = pl.DeviceIdType.MESH
bf16 = jnp.bfloat16
f32 = jnp.float32
LOG2E = math.log2(math.e)
highest_precision = lax.Precision.HIGHEST


def norm_rows(x, gain, eps):
    centred = x - jnp.mean(x, axis=-1, keepdims=True)
    spread = jnp.mean(centred * centred, axis=-1, keepdims=True)
    return centred * lax.rsqrt(spread + eps) * gain


def iota(shape, axis):
    return lax.broadcasted_iota(jnp.int32, shape, axis)


def dot(a, b):
    return jnp.dot(a, b, preferred_element_type=f32)


def exact_dot(a, b):
    return jnp.dot(a, b, preferred_element_type=f32, precision=highest_precision)


def gelu(x):
    return 0.5 * x * (1.0 + lax.erf(x * math.sqrt(0.5)))


def request_places(targets, owners):
    count = targets.shape[1]
    match = (iota((owners, count), 0) == targets).astype(f32)
    earlier = (iota((count, count), 0) < iota((count, count), 1)).astype(bf16)
    seen = dot(match.astype(bf16), earlier)
    return targets, jnp.sum(seen * match, axis=0, keepdims=True).astype(jnp.int32)


def partner(img, k):
    dx, dy, dc = k // 8, (k // 2) % 4, k % 2
    x, y, core = img // 8, (img // 2) % 4, img % 2
    return lax.rem(x + dx, 4) * 8 + lax.rem(y + dy, 4) * 2 + lax.rem(core + dc, 2)


def split(x):
    high = x.astype(bf16)
    return high, (x - high.astype(f32)).astype(bf16)


def trunk_kernel(
    tok_hbm, gain_ref, wqkv_hbm, wproj_hbm, wn1_hbm, g1_ref, wn2_hbm, g2_ref,
    req_ref, points_ref, pe_ref, bias_ref, dec_qkv_ref, dec_out_ref, dec_gains_ref,
    mlp1_hbm, mlp2_hbm, hyper_hbm, hyper_out_ref, up1_ref, up_gain_ref, up2_ref,
    chosen_hbm, mover_hbm,
    tok, wqkv, wproj, wn1, wn2, normed, loc, got, vrows, outs, att, maps, halo,
    load_sem, qkv_send, qkv_recv, out_send, out_recv, halo_send, halo_recv,
    emb_ref, outgoing, arrived, mlp1, mlp2, hyper, keys, values, mixed, level, got_mixed, got_level, ups,
    ready, received, chooser, chosen, mover,
    late_sem, point_send, point_recv, stat_send, stat_recv, mask_send, mask_recv, leave_sem,
):
    me = lax.axis_index("tok")
    rows = tok.shape[0]
    two = 2 * HDIM
    slots = received.shape[1] * CAP
    contract = (((1,), (1,)), ((), ()))
    inner = HEADS * HDIM
    tile = 256
    tiles = rows // tile
    qblock = 512

    loads = [
        pltpu.make_async_copy(tok_hbm.at[pl.ds(i * tile, tile)], tok.at[pl.ds(i * tile, tile)], load_sem.at[i])
        for i in range(tiles)
    ]
    columns = [pl.ds(kind * inner, inner) for kind in range(3)]
    weights_in = [
        pltpu.make_async_copy(wqkv_hbm.at[:, columns[kind]], wqkv.at[:, columns[kind]], load_sem.at[11 + kind])
        for kind in range(3)
    ]
    loads.append(weights_in[1])
    loads.append(pltpu.make_async_copy(wn1_hbm, wn1, load_sem.at[5]))
    loads.append(pltpu.make_async_copy(wn2_hbm, wn2, load_sem.at[6]))
    loads.append(weights_in[2])
    loads.append(weights_in[0])
    for d in range(RING):
        owner = lax.rem(me + d, RING)
        loads.append(
            pltpu.make_async_copy(
                wproj_hbm.at[pl.ds(pl.multiple_of(owner * two, 32), two)],
                wproj.at[pl.ds(d * two, two)],
                load_sem.at[7 + d],
            )
        )
    late = [
        pltpu.make_async_copy(a, b, late_sem.at[i])
        for i, (a, b) in enumerate(((mlp1_hbm, mlp1), (mlp2_hbm, mlp2), (hyper_hbm, hyper)))
    ]
    for load in loads + late:
        load.start()

    img = lax.axis_index("img")
    owners = received.shape[1]
    barrier = pltpu.get_barrier_semaphore()
    for d in range(1, RING):
        pl.semaphore_signal(
            barrier, inc=1, device_id={"tok": lax.rem(me + d, RING)}, device_id_type=MESH
        )

    @pl.loop(1, owners)
    def _(k):
        pl.semaphore_signal(barrier, inc=1, device_id={"img": partner(img, k)}, device_id_type=MESH)

    scale = math.log2(math.e) / math.sqrt(HDIM)

    def qkv_copy(kind, head, d):
        owner = lax.rem(me + d, RING)
        first = pl.multiple_of(kind * inner + owner * two + head * HDIM, 16)
        return pltpu.make_async_remote_copy(
            src_ref=loc.at[pl.ds(first, HDIM)],
            dst_ref=got.at[kind, head, d],
            send_sem=qkv_send.at[kind, head, d],
            recv_sem=qkv_recv.at[kind, head, d],
            device_id={"tok": owner},
            device_id_type=MESH,
        )

    def project(kind, first, last):
        @pl.loop(first, last)
        def _(i):
            span = pl.ds(pl.multiple_of(i * tile, tile), tile)
            part = jnp.dot(
                normed[span, :], wqkv[:, kind * inner : (kind + 1) * inner], preferred_element_type=f32
            )
            if kind == 0:
                part = part * scale
            loc[kind * inner : (kind + 1) * inner, span] = part.astype(bf16).T

    def early_keys(d, part):
        owner = lax.rem(me + d, RING)
        first = pl.multiple_of(inner + owner * two, 16)
        span = pl.ds(part * (rows // 2), rows // 2)
        return pltpu.make_async_remote_copy(
            src_ref=loc.at[pl.ds(first, HDIM), span],
            dst_ref=got.at[1, 0, d, :, span],
            send_sem=qkv_send.at[1, 0, d],
            recv_sem=qkv_recv.at[1, 0, d],
            device_id={"tok": owner},
            device_id_type=MESH,
        )

    for part in range(2):
        for i in range(part * tiles // 2, (part + 1) * tiles // 2):
            loads[i].wait()
            span = pl.ds(i * tile, tile)
            normed[span, :] = norm_rows(tok[span, :].astype(f32), gain_ref[...].reshape(1, -1), 1e-06).astype(bf16)
        if part == 0:
            weights_in[1].wait()
        project(1, part * tiles // 2, (part + 1) * tiles // 2)
        if part == 0:
            pl.semaphore_wait(barrier, owners - 1 + RING - 1)
        for d in (1, 3, 2):
            early_keys(d, part).start()
    for kind in (2, 0):
        weights_in[kind].wait()
        project(kind, 0, tiles)
        for d in (1, 3, 2):
            qkv_copy(kind, 0, d).start()
    for kind in (1, 2, 0):
        for d in (1, 3, 2):
            qkv_copy(kind, 1, d).start()
    place = request_places(req_ref[...], owners)
    placing = (iota((owners * 8, slots // 2), 0) == place[0] * 8 + place[1]).astype(bf16)
    line = iota((128, slots // 2), 0)
    across, down = points_ref[0:1, :], points_ref[1:2, :]
    parts = jnp.where(
        line == 0,
        across // 32,
        jnp.where(line == 1, across % 32, jnp.where(line == 2, down // 32, jnp.where(line == 3, down % 32, 0))),
    )
    outgoing[...] = lax.dot_general(
        placing, parts.astype(f32).astype(bf16), contract, preferred_element_type=f32
    ).reshape(owners, 8, 128)

    def point_copy(k):
        to = partner(img, k)
        return pltpu.make_async_remote_copy(
            src_ref=outgoing.at[to], dst_ref=arrived.at[img],
            send_sem=point_send.at[k], recv_sem=point_recv.at[k],
            device_id={"img": to}, device_id_type=MESH,
        )

    for kind in range(3):
        for head in range(2):
            first = pl.multiple_of(kind * inner + me * two + head * HDIM, 16)
            got[kind, head, 0] = loc[pl.ds(first, HDIM), :]

    @pl.loop(1, owners)
    def _(k):
        point_copy(k).start()
    arrived[img] = outgoing[img]

    def out_copy(head, d):
        target = lax.rem(me - d + RING, RING)
        return pltpu.make_async_remote_copy(
            src_ref=outs.at[head, d],
            dst_ref=att.at[d, pl.ds(pl.multiple_of(head * HDIM, 16), HDIM)],
            send_sem=out_send.at[head, d],
            recv_sem=out_recv.at[head, d],
            device_id={"tok": target},
            device_id_type=MESH,
        )

    filler = (lax.broadcasted_iota(jnp.int32, (48, rows), 0) == 0).astype(bf16)
    halves = rows // qblock

    @pl.loop(0, 2)
    def _(head):
        for d in range(1, RING):
            qkv_copy(1, head, d).wait_recv()
            qkv_copy(2, head, d).wait_recv()
        for d in range(RING):
            vrows[d] = jnp.concatenate([got[2, head, d], filler], axis=0).T

        @pl.loop(0, RING)
        def _(turn):
            slot = lax.rem(turn + head, RING)

            @pl.when(slot > 0)
            def _():
                qkv_copy(0, head, slot).wait_recv()

            @pl.loop(0, halves)
            def _(half):
                span = pl.ds(pl.multiple_of(half * qblock, qblock), qblock)
                query = got[0, head, slot, :, span].T

                def scores(d):
                    return jnp.dot(query, got[1, head, d], preferred_element_type=f32)

                now = scores(0)
                top = None
                for d in range(RING):
                    ahead = scores(d + 1) if d + 1 < RING else None
                    here = jnp.max(now, axis=1, keepdims=True)
                    fresh = here if top is None else jnp.maximum(top, here)
                    weights = jnp.exp2(now - fresh).astype(bf16)
                    part = jnp.dot(weights, vrows[d], preferred_element_type=f32)
                    total = part if top is None else total * jnp.exp2(top - fresh) + part
                    top, now = fresh, ahead
                final = (total * (1.0 / total[:, HDIM : HDIM + 1])).astype(bf16).T[:HDIM]
                outs[head, slot, :, span] = final

            @pl.when(slot > 0)
            def _():
                out_copy(head, slot).start()

            @pl.when(slot == 0)
            def _():
                att[0, pl.ds(pl.multiple_of(head * HDIM, 16), HDIM), :] = outs[head, 0]

    for d in range(1, RING):
        for head in range(2):
            out_copy(head, d).wait_recv()
    for load in loads[5:7] + loads[9:]:
        load.wait()

    def halo_copy(side):
        start = GRID + (0 if side == 0 else rows - GRID)
        return pltpu.make_async_remote_copy(
            src_ref=maps.at[1, pl.ds(start, GRID)],
            dst_ref=halo.at[side],
            send_sem=halo_send.at[side],
            recv_sem=halo_recv.at[side],
            device_id={"tok": lax.rem(me + (RING - 1 if side == 0 else 1), RING)},
            device_id_type=MESH,
        )

    def spread_columns(plain, at):
        count = plain.shape[0]
        column = lax.broadcasted_iota(jnp.int32, (count, NECK), 0) % GRID
        maps[1, at, :] = plain.astype(bf16)
        maps[0, at, :] = jnp.where(column == 0, 0.0, pltpu.roll(plain, 1, 0)).astype(bf16)
        maps[2, at, :] = jnp.where(column == GRID - 1, 0.0, pltpu.roll(plain, count - 1, 0)).astype(bf16)

    def narrow_tile(i):
        span = pl.ds(pl.multiple_of(i * tile, tile), tile)
        mixed = jnp.concatenate(
            [att[d, :, span] for d in range(RING)], axis=0
        ).T
        block = tok[span, :].astype(f32) + jnp.dot(mixed, wproj[...], preferred_element_type=f32)
        thin = jnp.dot(block.astype(bf16), wn1[...], preferred_element_type=f32)
        thin = norm_rows(thin, g1_ref[...], 1e-06).astype(bf16).astype(f32)
        spread_columns(thin, pl.ds(pl.multiple_of(GRID + i * tile, GRID), tile))

    @pl.loop(0, 2)
    def _(i):
        narrow_tile(i * (tiles - 1))
    halo_copy(0).start()
    halo_copy(1).start()
    @pl.loop(1, tiles - 1)
    def _(i):
        narrow_tile(i)

    def conv_tile(i):
        total = None
        for row_off in range(3):
            at = pl.ds(pl.multiple_of(i * tile + row_off * GRID, GRID), tile)
            for col_off in range(3):
                tap = (row_off * 3 + col_off) * NECK
                part = jnp.dot(maps[col_off, at, :], wn2[tap : tap + NECK, :], preferred_element_type=f32)
                total = part if total is None else total + part
        emb_ref[pl.ds(pl.multiple_of(i * tile, tile), tile), :] = norm_rows(
            total, g2_ref[...], 1e-06
        )

    @pl.loop(1, tiles - 1)
    def _(i):
        conv_tile(i)

    halo_copy(0).wait_recv()
    halo_copy(1).wait_recv()
    above = halo[1].astype(f32) * (me > 0).astype(f32)
    below = halo[0].astype(f32) * (me < RING - 1).astype(f32)
    spread_columns(above, pl.ds(0, GRID))
    spread_columns(below, pl.ds(GRID + rows, GRID))

    @pl.loop(0, 2)
    def _(i):
        conv_tile(i * (tiles - 1))

    for kind in range(3):
        for head in range(2):
            for d in range(1, RING):
                qkv_copy(kind, head, d).wait_send()
    for head in range(2):
        for d in range(1, RING):
            out_copy(head, d).wait_send()
    halo_copy(0).wait_send()
    halo_copy(1).wait_send()
    width = ATTN_DIM // DEC_HEADS
    turn = 2.0 * math.pi
    px_row, py_row = pe_ref[0:1, :], pe_ref[1:2, :]
    grid_rows = rows // GRID
    col_angle = turn * (((iota((GRID, 128), 0).astype(f32) + 0.5) / GRID * 2.0 - 1.0) * px_row)
    row_no = iota((grid_rows, 128), 0) + me * grid_rows
    row_angle = turn * (((row_no.astype(f32) + 0.5) / GRID * 2.0 - 1.0) * py_row)
    col_sin, col_cos = jnp.sin(col_angle), jnp.cos(col_angle)
    row_sin, row_cos = jnp.sin(row_angle), jnp.cos(row_angle)
    key_w = dec_qkv_ref[1]
    value_w = dec_qkv_ref[2].astype(bf16)
    key_high, key_low = split(key_w)
    codes = []
    for r in range(grid_rows):
        rs, rc = row_sin[r : r + 1], row_cos[r : r + 1]
        codes.append(
            jnp.concatenate([col_sin * rc + col_cos * rs, col_cos * rc - col_sin * rs], axis=1)
        )
    cell = emb_ref[...]
    high, low = split(cell + jnp.concatenate(codes, axis=0))
    both = dot(high, jnp.concatenate([key_high, key_low], axis=1))
    k_high, k_low = split(both[:, 0:128] + (both[:, 128:256] + dot(low, key_high)))
    keys[:, 0:128] = k_high
    keys[:, 128:256] = k_low
    values[...] = dot(cell.astype(bf16), value_w).astype(bf16)

    @pl.loop(1, owners)
    def _(k):
        point_copy(k).wait_recv()

    row = iota((slots, owners * 8), 0)
    pick = (iota((slots, owners * 8), 1) == (row // CAP) * 8 + row % CAP).astype(bf16)
    picked = dot(pick, arrived[...].reshape(owners * 8, 128).astype(bf16))
    where_x = picked[:, 0:1] * 32.0 + picked[:, 1:2]
    where_y = picked[:, 2:3] * 32.0 + picked[:, 3:4]
    angle = turn * (
        ((where_x + 0.5) / IMG_SIDE * 2.0 - 1.0) * px_row + ((where_y + 0.5) / IMG_SIDE * 2.0 - 1.0) * py_row
    )
    query_tok = bias_ref[...] + jnp.concatenate([jnp.sin(angle), jnp.cos(angle)], axis=1)
    query = exact_dot(query_tok, dec_qkv_ref[0]) * (LOG2E / math.sqrt(width))
    head_of = iota((slots, 128), 1) // width
    mix = jnp.zeros((slots, 128), f32)
    lev = jnp.zeros((slots, 128), f32)
    group = 4
    for first in range(0, DEC_HEADS, group):
        heads = range(first, first + group)
        q_high, q_low = split(jnp.concatenate([jnp.where(head_of == e, query, 0.0) for e in heads], axis=0))
        scores = lax.dot_general(
            jnp.concatenate([q_high, q_high], axis=1), keys[...], contract, preferred_element_type=f32
        ) + lax.dot_general(q_low, keys[:, 0:128], contract, preferred_element_type=f32)
        top = jnp.max(scores, axis=1, keepdims=True)
        weights = jnp.exp2(scores - top)
        total = jnp.sum(weights, axis=1, keepdims=True)
        part = dot(weights.astype(bf16), values[...]) / total
        height = top + jnp.log(total) * LOG2E
        for j, e in enumerate(heads):
            at = slice(j * slots, (j + 1) * slots)
            mix = jnp.where(head_of == e, part[at], mix)
            lev = jnp.where(head_of == e, height[at], lev)
    mixed[...] = mix.astype(bf16)
    level[...] = lev

    def stat_copy(kind, d):
        src, dst = ((mixed, got_mixed), (level, got_level))[kind]
        return pltpu.make_async_remote_copy(
            src_ref=src, dst_ref=dst.at[d],
            send_sem=stat_send.at[kind, d], recv_sem=stat_recv.at[kind, d],
            device_id={"tok": lax.rem(me + d, RING)}, device_id_type=MESH,
        )

    for d in (2, 1, 3):
        stat_copy(0, d).start()
        stat_copy(1, d).start()

    gain_col = jnp.sum(
        jnp.where(iota((UP1, UP1), 0) == iota((UP1, UP1), 1), up_gain_ref[...], 0.0), axis=1, keepdims=True
    )
    first_w = up1_ref[...].T.astype(bf16)
    second_w = up2_ref[...].T.astype(bf16)
    lanes = 256

    @pl.loop(0, rows // lanes)
    def _(i):
        span = pl.ds(pl.multiple_of(i * lanes, lanes), lanes)
        wide = lax.dot_general(
            first_w, emb_ref[span, :].astype(bf16), contract, preferred_element_type=f32
        )
        for g in range(4):
            part = wide[g * UP1 : (g + 1) * UP1]
            centred = part - jnp.mean(part, axis=0, keepdims=True)
            spread = jnp.mean(centred * centred, axis=0, keepdims=True)
            first = gelu(centred * lax.rsqrt(spread + 1e-06) * gain_col)
            ups[g, :, span] = gelu(dot(second_w, first.astype(bf16))).astype(bf16)

    for load in late:
        load.wait()
    mlp1_w, mlp2_w = mlp1[...].astype(bf16), mlp2[...].astype(bf16)
    hyper_w = [hyper[i].astype(bf16) for i in range(2)]
    for d in range(1, RING):
        stat_copy(0, d).wait_recv()
        stat_copy(1, d).wait_recv()
    levels = [lev] + [got_level[d] for d in range(1, RING)]
    parts = [mixed[...].astype(f32)] + [got_mixed[d].astype(f32) for d in range(1, RING)]
    peak = jnp.maximum(jnp.maximum(levels[0], levels[1]), jnp.maximum(levels[2], levels[3]))
    shares = [jnp.exp2(item - peak) for item in levels]
    cross = sum(s * p for s, p in zip(shares, parts)) / sum(shares)

    first_out = norm_rows(
        query_tok + dot(cross.astype(bf16), dec_out_ref[...].astype(bf16)), dec_gains_ref[0:1, :], 1e-05
    )
    hidden = jnp.maximum(dot(first_out.astype(bf16), mlp1_w), 0.0)
    second = norm_rows(
        first_out + dot(hidden.astype(bf16), mlp2_w), dec_gains_ref[1:2, :], 1e-05
    )
    vec = jnp.maximum(dot(second.astype(bf16), hyper_w[0]), 0.0)
    vec = jnp.maximum(dot(vec.astype(bf16), hyper_w[1]), 0.0)
    last = hyper_out_ref[...]
    vec = lax.dot_general(
        vec.astype(bf16), jnp.concatenate([last] * 4, axis=0).astype(bf16), contract, preferred_element_type=f32
    ).astype(bf16)
    big = owners * 16
    row = iota((big, slots), 0)
    repeat = (iota((big, slots), 1) == (row // 16) * CAP + row % CAP).astype(bf16)
    row = iota((big, 128), 0)
    stacked = jnp.where((row // CAP) % 4 == iota((big, 128), 1) // UP2, dot(repeat, vec), 0.0).astype(bf16)

    def mask_copy(g, k):
        to = partner(img, k)
        return pltpu.make_async_remote_copy(
            src_ref=ready.at[g, to], dst_ref=received.at[g, img],
            send_sem=mask_send.at[g, k], recv_sem=mask_recv.at[g, k],
            device_id={"img": to}, device_id_type=MESH,
        )

    for g in range(4):
        ready[g] = dot(stacked, ups[g]).astype(bf16).reshape(owners, 16, rows)

        @pl.loop(1, owners)
        def _(k):
            mask_copy(g, lax.rem(k * 13, owners)).start()
        received[g, img] = ready[g, img]

    half = slots // 2
    diagonal = iota((half, half), 0) == iota((half, half), 1)
    spot = jnp.sum(
        jnp.where(diagonal, (place[0] * 16 + place[1]).astype(f32), 0.0), axis=1, keepdims=True
    ).astype(jnp.int32)
    for k in range(4):
        chooser[k * half : (k + 1) * half, :] = (iota((half, owners * 16), 1) == spot + k * CAP).astype(bf16)
    row, col = iota((512, 512), 0), iota((512, 512), 1)
    inside = row % 128
    mover[...] = (col == (inside // GRID) * 256 + (inside % GRID) * 4 + row // 128).astype(bf16)

    @pl.loop(1, owners)
    def _(k):
        point_copy(k).wait_send()
    for d in range(1, RING):
        stat_copy(0, d).wait_send()
        stat_copy(1, d).wait_send()
    leaving = [pltpu.make_async_copy(mover, mover_hbm, leave_sem.at[4])]
    leaving[0].start()
    for g in range(4):
        @pl.loop(1, owners)
        def _(k):
            mask_copy(g, k).wait_recv()
        chosen[g] = dot(chooser[...], received[g].reshape(owners * 16, rows)).astype(bf16)
        leaving.append(pltpu.make_async_copy(chosen.at[g], chosen_hbm.at[g], leave_sem.at[g]))
        leaving[-1].start()
    for g in range(4):
        @pl.loop(1, owners)
        def _(k):
            mask_copy(g, k).wait_send()
    for copy in leaving:
        copy.wait()


def trunk(
    picture, ln_gain, w_qkv, w_proj, w_neck1, gain1, w_neck2, gain2, pe_matrix, query_bias, dec_qkv,
    dec_out, dec_gains, w_mlp1, w_mlp2, w_hyper, w_hyper_out, w_up1, up_gain, w_up2, req_image, points, owners,
):
    rows, width = picture.shape
    anywhere = pl.BlockSpec(memory_space=pl.ANY)
    local = pl.BlockSpec(memory_space=pltpu.VMEM)
    inner = HEADS * HDIM
    slots = owners * CAP
    dma = pltpu.SemaphoreType.DMA
    return pl.pallas_call(
        trunk_kernel,
        out_shape=(
            jax.ShapeDtypeStruct((4, slots * 2, rows), bf16),
            jax.ShapeDtypeStruct((512, 512), bf16),
        ),
        in_specs=[anywhere, local, anywhere, anywhere, anywhere, local, anywhere, local]
        + [local] * 7 + [anywhere] * 3 + [local] * 4,
        out_specs=(anywhere, anywhere),
        scratch_shapes=[
            pltpu.VMEM((rows, width), bf16),
            pltpu.VMEM(w_qkv.shape, bf16),
            pltpu.VMEM(w_proj.shape, bf16),
            pltpu.VMEM(w_neck1.shape, bf16),
            pltpu.VMEM(w_neck2.shape, bf16),
            pltpu.VMEM((rows, width), bf16),
            pltpu.VMEM((3 * inner, rows), bf16),
            pltpu.VMEM((3, 2, RING, HDIM, rows), bf16),
            pltpu.VMEM((RING, rows, 128), bf16),
            pltpu.VMEM((2, RING, HDIM, rows), bf16),
            pltpu.VMEM((RING, 2 * HDIM, rows), bf16),
            pltpu.VMEM((3, rows + 2 * GRID, NECK), bf16),
            pltpu.VMEM((2, GRID, NECK), bf16),
            dma((14,)),
            dma((3, 2, RING)),
            dma((3, 2, RING)),
            dma((2, RING)),
            dma((2, RING)),
            dma((2,)),
            dma((2,)),
            pltpu.VMEM((rows, NECK), f32),
            pltpu.VMEM((owners, 8, 128), f32),
            pltpu.VMEM((owners, 8, 128), f32),
            pltpu.VMEM(w_mlp1.shape, f32),
            pltpu.VMEM(w_mlp2.shape, f32),
            pltpu.VMEM(w_hyper.shape, f32),
            pltpu.VMEM((rows, 256), bf16),
            pltpu.VMEM((rows, 128), bf16),
            pltpu.VMEM((slots, 128), bf16),
            pltpu.VMEM((slots, 128), f32),
            pltpu.VMEM((RING, slots, 128), bf16),
            pltpu.VMEM((RING, slots, 128), f32),
            pltpu.VMEM((4, 128, rows), bf16),
            pltpu.VMEM((4, owners, 16, rows), bf16),
            pltpu.VMEM((4, owners, 16, rows), bf16),
            pltpu.VMEM((slots * 2, owners * 16), bf16),
            pltpu.VMEM((4, slots * 2, rows), bf16),
            pltpu.VMEM((512, 512), bf16),
            dma((3,)),
            dma((owners,)),
            dma((owners,)),
            dma((2, RING)),
            dma((2, RING)),
            dma((4, owners)),
            dma((4, owners)),
            dma((5,)),
        ],
        compiler_params=pltpu.CompilerParams(
            collective_id=0, has_side_effects=True, vmem_limit_bytes=62 * 1024 * 1024
        ),
    )(
        picture, ln_gain, w_qkv, w_proj, w_neck1, gain1.reshape(1, -1), w_neck2,
        gain2.reshape(1, -1), req_image.T, points.T, pe_matrix, query_bias.reshape(1, -1), dec_qkv,
        dec_out, dec_gains, w_mlp1, w_mlp2, w_hyper, w_hyper_out.T, w_up1, up_gain.reshape(1, -1), w_up2,
    )


def interleave_kernel(chosen_ref, mover_ref, out_ref):
    slots = out_ref.shape[0]
    sub = chosen_ref.shape[2] // 128
    sides = [
        jnp.concatenate(
            [
                chosen_ref[
                    dr * 2 + dc, (er * 2 + ec) * slots : (er * 2 + ec + 1) * slots, p * 128 : (p + 1) * 128
                ]
                for dc in range(2)
                for ec in range(2)
            ],
            axis=1,
        )
        for p in range(sub)
        for dr in range(2)
        for er in range(2)
    ]
    lines = dot(jnp.concatenate(sides, axis=0), mover_ref[...])
    for p in range(sub):
        for j in range(4):
            at = slice((p * 4 + j) * slots, (p * 4 + j + 1) * slots)
            for r in range(2):
                line = (p * 8 + r * 4 + j) * 256
                out_ref[:, line : line + 256] = lines[at, r * 256 : (r + 1) * 256]


def interleave(chosen, mover):
    groups, tall, rows = chosen.shape
    slots = tall // 4
    lanes = 256
    return pl.pallas_call(
        interleave_kernel,
        out_shape=jax.ShapeDtypeStruct((slots, rows * 16), f32),
        grid=(rows // lanes,),
        in_specs=[
            pl.BlockSpec((groups, tall, lanes), lambda i: (0, 0, i)),
            pl.BlockSpec((512, 512), lambda i: (0, 0)),
        ],
        out_specs=pl.BlockSpec((slots, lanes * 16), lambda i: (0, i)),
        compiler_params=pltpu.CompilerParams(vmem_limit_bytes=56 * 1024 * 1024),
    )(chosen, mover)


def body(tokens, *others):
    return interleave(*trunk(tokens[0], *others, lax.axis_size("img")))


def solution(mesh):
    placed = (
        P("img", "tok", None),
        P(),
        P(),
        P(),
        P(),
        P(),
        P(),
        P(),
        P(),
        P(),
        P(),
        P(),
        P(),
        P(),
        P(),
        P(),
        P(),
        P(),
        P(),
        P(),
        P("img", None),
        P("img", None),
    )
    return jax.shard_map(
        body, mesh=mesh, in_specs=placed, out_specs=P("img", "tok"), check_vma=False
    )
```
